32 devices in a mesh: expert: 8 (over y, x, core), dp: 4 (over z).
Axes of the slice: x: 2, y: 2, z: 4, core: 2. Of those that a mesh axis runs over, the one named last changes fastest.
Arguments:
- tokens: bfloat16 [4096, 2048], P(('expert', 'dp')), may hold values from -6 to 6
- expert_ids: int32 [4096, 8], P(('expert', 'dp')), may hold values from 0 to 15, all different within a row; in each aligned block of 128 rows (0 to 127, 128 to 255, ...) at most 72 rows name the same one
- router: bfloat16 [2048, 16], replicated, may hold values from -0.25 to 0.25
- w_gate: bfloat16 [16, 2048, 640], P('expert'), may hold values from -0.125 to 0.125
- w_up: bfloat16 [16, 2048, 640], P('expert'), may hold values from -0.125 to 0.125
- w_down: bfloat16 [16, 640, 2048], P('expert'), may hold values from -1 to 1
- out_grad: bfloat16 [4096, 2048], P(('expert', 'dp')), may hold values from -6 to 6
Outputs:
- mixed: bfloat16 [4096, 2048], P(('expert', 'dp'))
- token_grad: bfloat16 [4096, 2048], P(('expert', 'dp'))
- router_grad: float32 [2048, 16], replicated
- gate_grad: bfloat16 [16, 2048, 640], P('expert', 'dp')
- up_grad: bfloat16 [16, 2048, 640], P('expert', 'dp')
- down_grad: bfloat16 [16, 640, 2048], P('expert', None, 'dp')
The draws below stay inside these ranges and needn't reach their ends.
Inputs may be any that keep to these rules, and one draw needn't show every extreme that they name: `expert_ids`: each row names 8 different experts; within the 128 rows of one device no expert is named more than 72 times.
All inputs are finite; a program needn't handle non-finite values.
Results may differ from the reference program's by a relative error of at most 0.008.
Values may be sent and summed in bfloat16 or wider, within the bound.
No kernel may reach another device: no remote copies, remote signals or barrier semaphores. Data moves between devices by JAX's collectives and lax.ppermute only.
A program may use at most 256 MiB of HBM per device.

```python
import math
import jax
import jax.numpy as jnp
import numpy as np
from jax import lax

D = 2048
FF = 640
TOPK = 8
TOK_DEV = 128
EXPERTS = 16
CAP = 72
TOKENS = 4096
N_EXPERT = 8
N_DP = 4


def steps_of(key, extent, shards, least, largest):
    factor_of = 1.0
    for dim, parts in shards:
        draws = jax.random.uniform(jax.random.fold_in(jax.random.fold_in(key, 6), dim), (parts,), jnp.float32, least / len(shards), largest / len(shards))
        factor_of = factor_of * jnp.repeat(jnp.exp(draws), extent[dim] // parts).reshape((-1,) + (1,) * (len(extent) - 1 - dim))
    return factor_of


def assign_block(rng, own, number, rows, count, top, reach, skew):
    sequence = jax.random.permutation(rng, count)
    crowded, usual = portions_of(count, rows * top, reach, skew, True), portions_of(count, rows * top, reach, skew, False)
    places = jnp.arange(count)

    def named(tallies, turn):
        used = int((tallies > 0).sum())
        fixed = max(1, used // 4)
        moved = fixed + (places - fixed + turn * (used - fixed)) % max(1, count - fixed)
        return jnp.zeros((count,), jnp.int32).at[sequence[jnp.where(places < fixed, places, moved)]].set(jnp.asarray(tallies, jnp.int32))

    tallies = jnp.where(number % 4 == 0, named(crowded, number // 4), named(usual, number - number // 4 - 1))
    mixed = jax.random.permutation(jax.random.fold_in(own, 3), count)
    giver, receiver = mixed[0:count // 2 * 2:2], mixed[1:count // 2 * 2:2]
    margin = jnp.minimum(tallies[giver] - 1, reach - tallies[receiver]) // 2
    margin = jnp.where((giver == sequence[0]) | (receiver == sequence[0]) | (tallies[receiver] == 0), 0, jnp.maximum(margin, 0))
    moved = jax.random.randint(jax.random.fold_in(own, 4), (count // 2,), 0, 1 << 20) % (margin + 1)
    tallies = tallies.at[giver].add(-moved).at[receiver].add(moved)
    members = jnp.searchsorted(jnp.cumsum(tallies), jnp.arange(rows * top), side="right").astype(jnp.int32)
    listing = members.reshape(top, rows).T
    listing = listing[jax.random.permutation(jax.random.fold_in(own, 1), rows)]
    turn = jax.random.randint(jax.random.fold_in(own, 2), (rows, 1), 0, top)
    return jnp.take_along_axis(listing, (jnp.arange(top)[None, :] + turn) % top, axis=1)


def portions_of(count, total, limit, skew, full):
    loads = [(1 << 20) // math.isqrt(grade ** skew) + 1 for grade in range(1, count + 1)]
    largest = limit if full else min(limit, max(-(-total // count), total * loads[0] // sum(loads)))
    least = 1 if total - largest >= count - 1 else 0
    holding, surplus = [largest] + [least] * (count - 1), total - largest - least * (count - 1)
    while surplus > 0:
        candidates = [i for i in range(1, count) if holding[i] < largest] or [i for i in range(1, count) if holding[i] < limit]
        whole, remaining = sum([loads[i] for i in candidates]), surplus
        for i in candidates:
            extra = min(limit - holding[i], max(1, remaining * loads[i] // whole), surplus)
            holding[i] = holding[i] + extra
            surplus = surplus - extra
    return np.array(holding)


def gaussian(stream_key, shape, spread, bound, split=(), kind=jnp.bfloat16):
    entries = spread * jax.random.normal(stream_key, shape, jnp.float32)
    if split:
        entries = entries * steps_of(stream_key, shape, split, -0.22, 0.18)
    return jnp.clip(entries, -bound, bound).astype(kind)


def setup_inputs(seed: int = 0) -> dict:
    keys = jax.random.split(jax.random.key(seed), 8)
    tokens = gaussian(keys[0], (TOKENS, D), 1.0, 6.0, ((0, 32),))
    expert_ids_keys = jax.random.split(jax.random.fold_in(keys[1], 1), TOKENS // TOK_DEV)
    expert_ids_turns = jax.random.permutation(jax.random.fold_in(keys[1], 3), TOKENS // TOK_DEV)
    expert_ids = jax.vmap(lambda own, number: assign_block(jax.random.fold_in(keys[1], 2), own, number, TOK_DEV, EXPERTS, TOPK, CAP, 2))(expert_ids_keys, expert_ids_turns).reshape((TOKENS, TOPK))
    router = gaussian(keys[2], (D, EXPERTS), (D // 4) ** -0.5, 0.25)
    w_gate = gaussian(keys[3], (EXPERTS, D, FF), D ** -0.5, 0.125, ((0, 8),))
    w_up = gaussian(keys[4], (EXPERTS, D, FF), D ** -0.5, 0.125, ((0, 8),))
    w_down = gaussian(keys[5], (EXPERTS, FF, D), (FF // 16) ** -0.5, 1.0, ((0, 8),))
    out_grad = gaussian(keys[6], (TOKENS, D), 1.0, 6.0, ((0, 32),))
    return dict(tokens=tokens, expert_ids=expert_ids, router=router, w_gate=w_gate, w_up=w_up, w_down=w_down, out_grad=out_grad)


def reference(tokens, expert_ids, router, w_gate, w_up, w_down, out_grad):
    f32 = jnp.float32
    bf16 = jnp.bfloat16
    n_tok = tokens.shape[0]
    blocks = n_tok // TOK_DEV
    n_assign = n_tok * TOPK
    ladder = jnp.arange(EXPERTS, dtype=jnp.int32)
    block_ids = expert_ids.reshape(blocks, TOK_DEV * TOPK)
    onehot = (block_ids[:, :, None] == ladder[None, None, :]).astype(jnp.int32)
    rank = jnp.sum((jnp.cumsum(onehot, axis=1) - onehot) * onehot, axis=2)
    block_idx = jnp.arange(blocks, dtype=jnp.int32)[:, None]
    source = block_idx // N_DP
    group = block_idx % N_DP
    position = (group * N_EXPERT + source) * CAP + rank
    per_expert = N_DP * N_EXPERT * CAP
    table = jnp.full((EXPERTS, per_expert), n_assign, jnp.int32)
    table = table.at[block_ids.reshape(-1), position.reshape(-1)].set(jnp.arange(n_assign, dtype=jnp.int32))

    logits = jnp.dot(tokens, router, preferred_element_type=f32)
    scores = jax.nn.sigmoid(logits)
    chosen = jnp.take_along_axis(scores, expert_ids, axis=1)
    total = jnp.sum(chosen, axis=1, keepdims=True)
    gates = chosen / total
    gate_flat = jnp.concatenate([gates.reshape(-1), jnp.zeros((1,), f32)])
    tok_pad = jnp.concatenate([tokens, jnp.zeros((1, D), bf16)], axis=0)
    grad_pad = jnp.concatenate([out_grad, jnp.zeros((1, D), bf16)], axis=0)

    def step(carry, inputs):
        mixed_acc, input_acc, sens_acc = carry
        index, weight_g, weight_u, weight_d = inputs
        live = index < n_assign
        tok = jnp.where(live, index // TOPK, n_tok).astype(jnp.int32)
        gate_rows = gate_flat[index]
        rows = tok_pad[tok]
        pre_gate = jnp.dot(rows, weight_g, preferred_element_type=f32)
        pre_up = jnp.dot(rows, weight_u, preferred_element_type=f32)
        sig = jax.nn.sigmoid(pre_gate)
        silu_val = pre_gate * sig
        hidden = (silu_val * pre_up).astype(bf16)
        expert_out = jnp.dot(hidden, weight_d, preferred_element_type=f32).astype(bf16)
        mixed_acc = mixed_acc.at[tok].add(gate_rows[:, None] * expert_out.astype(f32))
        cot_rows = grad_pad[tok]
        sens = jnp.sum(cot_rows.astype(f32) * expert_out.astype(f32), axis=1)
        sens_acc = sens_acc.at[index].add(sens)
        row_grad = (gate_rows[:, None] * cot_rows.astype(f32)).astype(bf16)
        hidden_grad = jnp.dot(row_grad, weight_d.T, preferred_element_type=f32)
        gate_term = (hidden_grad * pre_up * sig * (1.0 + pre_gate * (1.0 - sig))).astype(bf16)
        up_term = (hidden_grad * silu_val).astype(bf16)
        input_grad = (jnp.dot(gate_term, weight_g.T, preferred_element_type=f32)
                      + jnp.dot(up_term, weight_u.T, preferred_element_type=f32)).astype(bf16)
        input_acc = input_acc.at[tok].add(input_grad.astype(f32))
        grad_g = jnp.dot(rows.T, gate_term, preferred_element_type=f32).astype(bf16)
        grad_u = jnp.dot(rows.T, up_term, preferred_element_type=f32).astype(bf16)
        grad_d = jnp.dot(hidden.T, row_grad, preferred_element_type=f32).astype(bf16)
        return (mixed_acc, input_acc, sens_acc), (grad_g, grad_u, grad_d)

    start = (jnp.zeros((n_tok + 1, D), f32), jnp.zeros((n_tok + 1, D), f32), jnp.zeros((n_assign + 1,), f32))
    final, grads = lax.scan(step, start, (table, w_gate, w_up, w_down))
    mixed_acc, input_acc, sens_acc = final
    mixed = mixed_acc[:n_tok].astype(bf16)
    gate_sens = sens_acc[:n_assign].reshape(n_tok, TOPK)
    chosen_grad = (gate_sens - jnp.sum(gate_sens * gates, axis=1, keepdims=True)) / total
    sel_grad = chosen_grad * chosen * (1.0 - chosen)
    pick = (expert_ids[:, :, None] == ladder[None, None, :]).astype(f32)
    logit_grad = jnp.einsum('tk,tke->te', sel_grad, pick).astype(bf16)
    token_grad = (input_acc[:n_tok] + jnp.dot(logit_grad, router.T, preferred_element_type=f32)).astype(bf16)
    router_grad = jnp.dot(tokens.T, logit_grad, preferred_element_type=f32)
    return (mixed, token_grad, router_grad, grads[0], grads[1], grads[2])
```

```python
import functools

import jax
import jax.numpy as jnp
from jax import lax
from jax.experimental import pallas as pl
from jax.experimental.pallas import tpu as pltpu
from jax.sharding import PartitionSpec as P

F32 = jnp.float32
BF16 = jnp.bfloat16
LANES = 128
PLANE = 8


def mm(a, b, contract):
    return lax.dot_general(a, b, (contract, ((), ())), preferred_element_type=F32)


NN = ((1,), (0,))
NT = ((1,), (1,))
TN = ((0,), (0,))


def expert_kernel(own, last, tok, width, ff, cols, units, *refs):
    refs = list(refs)
    scal = refs.pop(0)
    blocks = [refs.pop(0) for _ in units]
    wc, wd = refs.pop(0), refs.pop(0)
    acc_in = None if own else refs.pop(0)
    outs = [refs.pop(0) for _ in range(3 if last else 1)]
    if own:
        hid, gu, rp_out = (refs.pop(0) for _ in range(3))
    x_s, o_s, wc_s, wd_s, pre_s, q_s, gb, acc_s = (refs.pop(0) for _ in range(8))
    if own:
        a_s, sacc = refs.pop(0), refs.pop(0)
    else:
        hid, gu = refs.pop(0), refs.pop(0)
    sems = refs.pop(0)
    rows = PLANE * tok
    both = 2 * ff
    chunk_rows = pre_s.shape[0]
    first_expert = scal[0]
    zcol = pl.multiple_of(scal[1] * cols, LANES)
    tiles_e = ff // LANES

    taken = iter(range(64))
    x_copies, o_copies = [], []
    place = 2
    for ref, count in zip(blocks, units):
        for u in range(count):
            at = pl.ds(pl.multiple_of(scal[place] * tok, tok), tok)
            place += 1
            base = 2 * tok * u
            x_copies.append(
                pltpu.make_async_copy(ref.at[pl.ds(base, tok), :], x_s.at[at, :], sems.at[next(taken)])
            )
            o_copies.append(
                pltpu.make_async_copy(
                    ref.at[pl.ds(base + tok, tok), pl.ds(0, width)], o_s.at[at, :], sems.at[next(taken)]
                )
            )

    def part(src, dst, lo, size):
        return pltpu.make_async_copy(
            src.at[:, pl.ds(lo, size)], dst.at[:, pl.ds(lo, size)], sems.at[next(taken)]
        )

    gate_copy = part(wc, wc_s, 0, both)
    up_copy = part(wc, wc_s, both, both + LANES)
    wd_copy = pltpu.make_async_copy(wd, wd_s, sems.at[next(taken)])
    acc_copies = []
    if not own:
        acc_copies = [pltpu.make_async_copy(acc_in, acc_s, sems.at[next(taken)])]
    for copy in [*x_copies, gate_copy, up_copy, *o_copies, wd_copy, *acc_copies]:
        copy.start()
    out_sem = next(taken)
    for copy in [*x_copies, gate_copy, up_copy]:
        copy.wait()

    lane = lax.broadcasted_iota(jnp.int32, (chunk_rows, LANES), 1)

    def chunk(c, carry):
        here = pl.ds(pl.multiple_of(c * chunk_rows, chunk_rows), chunk_rows)
        pre_s[...] = mm(x_s[here, :width], wc_s[...], NN)

        @pl.when(c == 0)
        def _():
            for copy in [*o_copies, wd_copy]:
                copy.wait()

        q_s[...] = mm(o_s[here, :], wd_s[...], NT)
        score = jax.nn.sigmoid(pre_s[:, 2 * both :])
        chosen = score * x_s[here, width:].astype(F32)
        gates = chosen / jnp.sum(chosen, axis=1, keepdims=True)
        for j in range(2):
            col = jnp.sum(jnp.where(lane == first_expert + j, gates, 0.0), axis=1, keepdims=True)
            gb[j, here, :] = jnp.broadcast_to(col, (chunk_rows, LANES))
        if own:
            a_s[here, :] = gates * (1.0 - score)
            sacc[:, here, :] = jnp.zeros((2, chunk_rows, LANES), F32)

        def piece(i, carry):
            r = pl.ds(pl.multiple_of(i * LANES, LANES), LANES)
            ra = pl.ds(pl.multiple_of(c * chunk_rows + i * LANES, LANES), LANES)
            for t in range(both // LANES):
                expert = t // tiles_e
                gate = gb[expert, ra, :]
                pre = pre_s[r, t * LANES : (t + 1) * LANES]
                up = pre_s[r, both + t * LANES : both + (t + 1) * LANES]
                q = q_s[r, t * LANES : (t + 1) * LANES]
                sig = 0.5 * jnp.tanh(0.5 * pre) + 0.5
                silu = pre * sig
                h = silu * up
                gq = gate * q
                hid[ra, t * LANES : (t + 1) * LANES] = (gate * h).astype(BF16)
                gu[ra, t * LANES : (t + 1) * LANES] = (gq * up * (sig + silu * (1.0 - sig))).astype(BF16)
                gu[ra, both + t * LANES : both + (t + 1) * LANES] = (gq * silu).astype(BF16)
                if own:
                    sacc[expert, ra, :] += h * q
            return carry

        lax.fori_loop(0, chunk_rows // LANES, piece, 0)
        return carry

    lax.fori_loop(0, rows // chunk_rows, chunk, 0)

    for copy in acc_copies:
        copy.wait()
    def weight_grad(i, grad):
        if not own:
            grad = grad + acc_s[i]
        acc_s[i] = grad
        if not last:
            pltpu.make_async_copy(acc_s.at[i], outs[0].at[i], sems.at[out_sem + i]).start()

    def from_tokens(i, carry):
        part = pl.ds(pl.multiple_of(i * both, LANES), both)
        weight_grad(i, mm(x_s[:, pl.ds(zcol, cols)], gu[:, part], TN))
        return carry

    lax.fori_loop(0, 2, from_tokens, 0)
    weight_grad(2, mm(o_s[:, pl.ds(zcol, cols)], hid[...], TN))
    if last:
        for i in range(2):
            for e in range(2):
                outs[i][e] = acc_s[i, :, e * ff : (e + 1) * ff].astype(BF16)
        for e in range(2):
            outs[2][e] = acc_s[2, :, e * ff : (e + 1) * ff].T.astype(BF16)

    if own:
        lane = lax.broadcasted_iota(jnp.int32, (rows, LANES), 1)
        term = jnp.zeros((rows, LANES), F32)
        shared = jnp.zeros((rows, LANES), F32)
        for j in range(2):
            sens = jnp.sum(sacc[j], axis=1, keepdims=True)
            term = term + jnp.where(lane == first_expert + j, sens, 0.0)
            shared = shared + gb[j] * sens
        grad = a_s[...] * (term - shared)
        high = grad.astype(BF16)
        low = (grad - high.astype(F32)).astype(BF16)
        gu[:, 2 * both : 2 * both + LANES] = high
        gu[:, 2 * both + LANES :] = low
        n_out = rp_out.shape[0]
        split = gu[:, 2 * both :]
        terms = mm(split, x_s[:, :width], TN)
        rp_out[...] = terms[:n_out] + terms[LANES : LANES + n_out]
    if not last:
        for i in range(3):
            pltpu.make_async_copy(acc_s.at[i], outs[0].at[i], sems.at[out_sem + i]).wait()


def expert_call(own, last, scal, blocks, wc, wd, acc, n_experts):
    tok = sum(b.shape[0] for b in blocks) // (2 * PLANE)
    units = tuple(b.shape[0] // (2 * tok) for b in blocks)
    both, width = wd.shape
    ff = both // 2
    cols = width // lax.axis_size("dp")
    rows = PLANE * tok
    anywhere = pl.BlockSpec(memory_space=pl.ANY)
    vmem = pl.BlockSpec(memory_space=pltpu.VMEM)
    args = [*blocks, wc, wd]
    if not own:
        args.append(acc)
    if last:
        out_shape = [jax.ShapeDtypeStruct((2, cols, ff), BF16)] * 2 + [jax.ShapeDtypeStruct((2, ff, cols), BF16)]
        out_specs = [vmem] * 3
    else:
        out_shape = [jax.ShapeDtypeStruct((3, cols, both), F32)]
        out_specs = [anywhere]
    if own:
        out_shape += [
            jax.ShapeDtypeStruct((rows, both), BF16),
            jax.ShapeDtypeStruct((rows, 2 * both + 2 * LANES), BF16),
            jax.ShapeDtypeStruct((n_experts, width), F32),
        ]
        out_specs += [vmem] * 3
    chunk = rows // 4
    scratch = [
        pltpu.VMEM((rows, width + LANES), BF16),
        pltpu.VMEM((rows, width), BF16),
        pltpu.VMEM((width, 2 * both + LANES), BF16),
        pltpu.VMEM((both, width), BF16),
        pltpu.VMEM((chunk, 2 * both + LANES), F32),
        pltpu.VMEM((chunk, both), F32),
        pltpu.VMEM((2, rows, LANES), F32),
        pltpu.VMEM((3, cols, both), F32),
    ]
    if own:
        scratch += [pltpu.VMEM((rows, LANES), F32), pltpu.VMEM((2, rows, LANES), F32)]
    else:
        scratch += [pltpu.VMEM((rows, both), BF16), pltpu.VMEM((rows, 2 * both), BF16)]
    scratch.append(pltpu.SemaphoreType.DMA((2 * PLANE + 7,)))
    aliases = {} if own or last else {1 + len(blocks) + 2: 0}
    flops = 2 * rows * width * both * 3 + 2 * rows * cols * both * 3
    return pl.pallas_call(
        functools.partial(expert_kernel, own, last, tok, width, ff, cols, units),
        grid_spec=pltpu.PrefetchScalarGridSpec(
            num_scalar_prefetch=1,
            grid=(),
            in_specs=[anywhere] * len(args),
            out_specs=out_specs,
            scratch_shapes=scratch,
        ),
        out_shape=out_shape,
        input_output_aliases=aliases,
        compiler_params=pltpu.CompilerParams(vmem_limit_bytes=58 * 1024 * 1024),
        cost_estimate=pl.CostEstimate(flops=flops, bytes_accessed=40_000_000, transcendentals=rows * both),
        name="experts_own" if own else "experts_last" if last else "experts_mid",
    )(scal, *args)


def flip(x, even, odd):
    groups = lax.axis_size("expert")
    return lax.ppermute(x, "expert", [(i, i ^ (odd if i % 2 else even)) for i in range(groups)])


def dense_body(tokens, expert_ids, router, w_gate, w_up, w_down, out_grad):
    tok, width = tokens.shape
    n_experts = router.shape[1]
    ff = w_gate.shape[2]
    n_dp = lax.axis_size("dp")
    me = lax.axis_index("expert")
    core = me % 2
    ladder = jnp.arange(LANES, dtype=jnp.int32)
    mask = jnp.any(expert_ids[:, :, None] == ladder[None, None, :], axis=1).astype(BF16)
    block = jnp.concatenate(
        [
            jnp.concatenate([tokens, mask], axis=1),
            jnp.concatenate([out_grad, jnp.zeros((tok, LANES), BF16)], axis=1),
        ],
        axis=0,
    )
    router_pad = jnp.pad(router, ((0, 0), (0, LANES - n_experts)))
    wc = jnp.concatenate([w_gate[0], w_gate[1], w_up[0], w_up[1], router_pad, router_pad], axis=1)
    wd = w_down.reshape(2 * ff, width)
    near_at = me ^ jnp.where(core == 0, 2, 4)
    other_at = me ^ jnp.where(core == 0, 5, 3)
    scal = jnp.stack(
        [me * 2, lax.axis_index("dp"), me, me ^ 1, near_at, near_at ^ 1, other_at, other_at ^ 1, me ^ 6, me ^ 7]
    ).astype(jnp.int32)
    ring = [(i, (i + 1) % n_dp) for i in range(n_dp)]

    def pair_of(b):
        return jnp.concatenate([b, flip(b, 1, 1)], axis=0)

    half = 2 * tok
    alone, pairs, nears, others, diagonals = ({} for _ in range(5))
    alone[0] = block
    alone[1] = lax.ppermute(block, "dp", ring)
    pairs[0] = pair_of(block)
    nears[0] = flip(pairs[0], 2, 4)
    pairs[1] = pair_of(alone[1])
    acc = None
    for g in range(-1, n_dp):
        if g + 1 < n_dp:
            diagonals[g + 1] = flip(nears[g + 1][:half], 4, 2)
            others[g + 1] = flip(nears[g + 1], 1, 1)
        if g + 2 < n_dp:
            nears[g + 2] = flip(pairs[g + 2], 2, 4)
        if g + 3 < n_dp:
            alone[g + 3] = lax.ppermute(alone[g + 2], "dp", ring)
        if g == 1:
            line = [rp] + [flip(rp, k, k) for k in (2, 4, 6)]
            part = jnp.dot(hid, wd, preferred_element_type=F32).astype(BF16)
            mixed = lax.psum_scatter(part, "expert", scatter_dimension=0, tiled=True)
            part = mm(gu, wc, NT).astype(BF16)
            token_grad = lax.psum_scatter(part, "expert", scatter_dimension=0, tiled=True)
        if g == 2:
            line = [rp] + [lax.ppermute(rp, "dp", [(i, i ^ k) for i in range(n_dp)]) for k in range(1, n_dp)]
        if g >= 0:
            out = expert_call(g == 0, g == n_dp - 1, scal, blocks, wc, wd, acc, n_experts)
            acc = out[0]
        if g + 1 == n_dp:
            break
        if g == 0:
            hid, gu, rp = out[1:]
        own_out = (hid, gu, rp) if g == 0 else tuple(line) if g > 0 else ()
        places = [(d, g + k) for d, k in ((diagonals, 1), (others, 1), (nears, 2), (alone, 3)) if g + k in d]
        held = list(lax.optimization_barrier((scal if g < 0 else acc, *own_out, *[d[k] for d, k in places])))
        if g < 0:
            scal = held.pop(0)
        else:
            acc = held.pop(0)
        own_out = [held.pop(0) for _ in own_out]
        if g == 0:
            hid, gu, rp = own_out
        elif g > 0:
            rp = (own_out[0] + own_out[1]) + (own_out[2] + own_out[3])
        for d, k in places:
            d[k] = held.pop(0)
        blocks = [pairs[g + 1], nears[g + 1], others[g + 1], diagonals[g + 1], flip(diagonals[g + 1], 1, 1)]
        if g + 3 < n_dp:
            pairs[g + 3] = pair_of(alone[g + 3])
        if g == 0:
            rp = rp + flip(rp, 1, 1)
    return (mixed, token_grad, rp.T, *out)


def flat_rows(array):
    return array.reshape(array.shape[0], array.shape[1] * array.shape[2], array.shape[3])


def sparse_body(tokens, expert_ids, router, w_gate, w_up, w_down, out_grad):
    f32 = jnp.float32
    bf16 = jnp.bfloat16
    tok_dev, width = tokens.shape
    top = expert_ids.shape[1]
    n_experts = router.shape[1]
    local_experts = w_gate.shape[0]
    groups = lax.axis_size("expert")
    capacity = (tok_dev * top * 9 + 8 * n_experts - 1) // (8 * n_experts)
    n_assign = tok_dev * top
    flat_ids = expert_ids.reshape(-1)
    ladder = jnp.arange(n_experts, dtype=jnp.int32)
    onehot = (flat_ids[:, None] == ladder[None, :]).astype(jnp.int32)
    rank = jnp.sum((jnp.cumsum(onehot, axis=0) - onehot) * onehot, axis=1)
    owner = flat_ids // local_experts
    within = flat_ids % local_experts
    dest = (within * groups + owner) * capacity + rank
    slot_src = jnp.full((n_experts * capacity,), n_assign, jnp.int32)
    slot_src = slot_src.at[dest].set(jnp.arange(n_assign, dtype=jnp.int32))
    live = slot_src < n_assign
    slot_tok = jnp.where(live, slot_src // top, 0)
    logits = jnp.dot(tokens, router, preferred_element_type=f32)
    scores = jax.nn.sigmoid(logits)
    chosen = jnp.take_along_axis(scores, expert_ids, axis=1)
    total = jnp.sum(chosen, axis=1, keepdims=True)
    gates = chosen / total
    gate_slots = jnp.where(live, gates.reshape(-1)[jnp.minimum(slot_src, n_assign - 1)], 0.0)
    send = jnp.where(live[:, None], tokens[slot_tok], jnp.zeros((), bf16))
    send = send.reshape(local_experts, groups, capacity, width)
    piece = lax.all_to_all(send, "expert", split_axis=1, concat_axis=1, tiled=True)
    shape = piece.shape
    rows = flat_rows(piece)
    pre_gate = jnp.einsum("jrd,jdf->jrf", rows, w_gate, preferred_element_type=f32)
    pre_up = jnp.einsum("jrd,jdf->jrf", rows, w_up, preferred_element_type=f32)
    hidden = (pre_gate * jax.nn.sigmoid(pre_gate) * pre_up).astype(bf16)
    expert_out = jnp.einsum("jrf,jfd->jrd", hidden, w_down, preferred_element_type=f32).astype(bf16)
    hid_shape = (shape[0], shape[1], shape[2], hidden.shape[2])
    expert_out = expert_out.reshape(shape)
    hidden = hidden.reshape(hid_shape)
    results = (expert_out, hidden, piece, pre_gate.reshape(hid_shape), pre_up.reshape(hid_shape))
    expert_out = results[0]
    hidden = flat_rows(results[1])
    back = lax.all_to_all(expert_out, "expert", split_axis=1, concat_axis=1, tiled=True).reshape(
        n_experts * capacity, width
    )
    picked = back[dest].reshape(tok_dev, top, width)
    mixed = jnp.einsum("tk,tkd->td", gates, picked.astype(f32)).astype(bf16)
    gate_sens = jnp.einsum("tkd,td->tk", picked, out_grad, preferred_element_type=f32)
    grad_rows = (gate_slots[:, None] * out_grad[slot_tok].astype(f32)).astype(bf16)
    grad_send = jnp.where(live[:, None], grad_rows, jnp.zeros((), bf16))
    grad_send = grad_send.reshape(local_experts, groups, capacity, width)
    grad_in4 = lax.all_to_all(grad_send, "expert", split_axis=1, concat_axis=1, tiled=True)
    grad_in = flat_rows(grad_in4)
    pre_gate = flat_rows(results[3])
    pre_up = flat_rows(results[4])
    hidden_grad = jnp.einsum("jrd,jfd->jrf", grad_in, w_down, preferred_element_type=f32)
    sig = jax.nn.sigmoid(pre_gate)
    silu_val = pre_gate * sig
    gate_term = (hidden_grad * pre_up * sig * (1.0 + pre_gate * (1.0 - sig))).astype(bf16)
    up_term = (hidden_grad * silu_val).astype(bf16)
    input_grad = (
        jnp.einsum("jrf,jdf->jrd", gate_term, w_gate, preferred_element_type=f32)
        + jnp.einsum("jrf,jdf->jrd", up_term, w_up, preferred_element_type=f32)
    ).astype(bf16)
    input_grad = input_grad.reshape(grad_in4.shape)
    returned = lax.all_to_all(
        input_grad, "expert", split_axis=1, concat_axis=1, tiled=True
    ).reshape(n_experts * capacity, width)
    moe_grad = jnp.sum(returned[dest].reshape(tok_dev, top, width).astype(f32), axis=1)
    chosen_grad = (gate_sens - jnp.sum(gate_sens * gates, axis=1, keepdims=True)) / total
    sel_grad = chosen_grad * chosen * (1.0 - chosen)
    pick = (expert_ids[:, :, None] == ladder[None, None, :]).astype(f32)
    logit_grad = jnp.einsum("tk,tke->te", sel_grad, pick).astype(bf16)
    token_grad = (moe_grad + jnp.dot(logit_grad, router.T, preferred_element_type=f32)).astype(bf16)
    router_grad = lax.psum(
        jnp.dot(tokens.T, logit_grad, preferred_element_type=f32), ("expert", "dp")
    )
    hidden_width = hidden.shape[2]
    arrived4 = results[2]
    columns = (
        lax.all_to_all(arrived4, "dp", split_axis=3, concat_axis=1, tiled=True),
        lax.all_to_all(grad_in4, "dp", split_axis=3, concat_axis=1, tiled=True),
    )
    hid_shape = (local_experts, groups, capacity, hidden_width)
    hiddens = (
        lax.all_gather(gate_term.reshape(hid_shape), "dp", axis=1, tiled=True),
        lax.all_gather(up_term.reshape(hid_shape), "dp", axis=1, tiled=True),
        lax.all_gather(results[1], "dp", axis=1, tiled=True),
    )
    x_cols = flat_rows(columns[0])
    g_cols = flat_rows(columns[1])
    gate_grad = jnp.einsum(
        "jrd,jrf->jdf", x_cols, flat_rows(hiddens[0]), preferred_element_type=f32
    ).astype(bf16)
    up_grad = jnp.einsum(
        "jrd,jrf->jdf", x_cols, flat_rows(hiddens[1]), preferred_element_type=f32
    ).astype(bf16)
    down_grad = jnp.einsum(
        "jrf,jrd->jfd", flat_rows(hiddens[2]), g_cols, preferred_element_type=f32
    ).astype(bf16)
    return (mixed, token_grad, router_grad, gate_grad, up_grad, down_grad)


def body(*args):
    plane = lax.axis_size("expert") == 8 and args[3].shape[0] == 2
    line = lax.axis_size("dp")
    return (dense_body if plane and line == 4 else sparse_body)(*args)


def solution(mesh):
    placed = (
        P(("expert", "dp"), None),
        P(("expert", "dp"), None),
        P(),
        P("expert", None, None),
        P("expert", None, None),
        P("expert", None, None),
        P(("expert", "dp"), None),
    )
    return jax.shard_map(
        body,
        mesh=mesh,
        in_specs=placed,
        out_specs=(
            P(("expert", "dp"), None),
            P(("expert", "dp"), None),
            P(),
            P("expert", "dp", None),
            P("expert", "dp", None),
            P("expert", None, "dp"),
        ),
        check_vma=False,
    )
```

```python
import functools

import jax
import jax.numpy as jnp
from jax import lax
from jax.experimental import pallas as pl
from jax.experimental.pallas import tpu as pltpu
from jax.sharding import PartitionSpec as P

F32 = jnp.float32
BF16 = jnp.bfloat16
LANES = 128
PLANE = 8


def mm(a, b, contract):
    return lax.dot_general(a, b, (contract, ((), ())), preferred_element_type=F32)


NN = ((1,), (0,))
NT = ((1,), (1,))
TN = ((0,), (0,))


def expert_kernel(own, last, tok, width, ff, cols, units, *refs):
    refs = list(refs)
    scal = refs.pop(0)
    blocks = [refs.pop(0) for _ in units]
    wc, wd = refs.pop(0), refs.pop(0)
    acc_in = None if own else refs.pop(0)
    outs = [refs.pop(0) for _ in range(3 if last else 1)]
    if own:
        hid, gu, rp_out = (refs.pop(0) for _ in range(3))
    x_s, o_s, wc_s, wd_s, pre_s, q_s, gb, acc_s = (refs.pop(0) for _ in range(8))
    if own:
        a_s, sacc = refs.pop(0), refs.pop(0)
    else:
        hid, gu = refs.pop(0), refs.pop(0)
    sems = refs.pop(0)
    rows = PLANE * tok
    both = 2 * ff
    chunk_rows = pre_s.shape[0]
    first_expert = scal[0]
    zcol = pl.multiple_of(scal[1] * cols, LANES)
    tiles_e = ff // LANES

    taken = iter(range(64))
    x_copies, o_copies = [], []
    place = 2
    for ref, count in zip(blocks, units):
        for u in range(count):
            at = pl.ds(pl.multiple_of(scal[place] * tok, tok), tok)
            place += 1
            base = 2 * tok * u
            x_copies.append(
                pltpu.make_async_copy(ref.at[pl.ds(base, tok), :], x_s.at[at, :], sems.at[next(taken)])
            )
            o_copies.append(
                pltpu.make_async_copy(
                    ref.at[pl.ds(base + tok, tok), pl.ds(0, width)], o_s.at[at, :], sems.at[next(taken)]
                )
            )

    def part(src, dst, lo, size):
        return pltpu.make_async_copy(
            src.at[:, pl.ds(lo, size)], dst.at[:, pl.ds(lo, size)], sems.at[next(taken)]
        )

    gate_copy = part(wc, wc_s, 0, both)
    up_copy = part(wc, wc_s, both, both + LANES)
    wd_copy = pltpu.make_async_copy(wd, wd_s, sems.at[next(taken)])
    acc_copies = []
    if not own:
        acc_copies = [pltpu.make_async_copy(acc_in, acc_s, sems.at[next(taken)])]
    for copy in [*x_copies, gate_copy, up_copy, *o_copies, wd_copy, *acc_copies]:
        copy.start()
    out_sem = next(taken)
    for copy in [*x_copies, gate_copy, up_copy]:
        copy.wait()

    lane = lax.broadcasted_iota(jnp.int32, (chunk_rows, LANES), 1)

    def chunk(c, carry):
        here = pl.ds(pl.multiple_of(c * chunk_rows, chunk_rows), chunk_rows)
        pre_s[...] = mm(x_s[here, :width], wc_s[...], NN)

        @pl.when(c == 0)
        def _():
            for copy in [*o_copies, wd_copy]:
                copy.wait()

        q_s[...] = mm(o_s[here, :], wd_s[...], NT)
        score = jax.nn.sigmoid(pre_s[:, 2 * both :])
        chosen = score * x_s[here, width:].astype(F32)
        gates = chosen / jnp.sum(chosen, axis=1, keepdims=True)
        for j in range(2):
            col = jnp.sum(jnp.where(lane == first_expert + j, gates, 0.0), axis=1, keepdims=True)
            gb[j, here, :] = jnp.broadcast_to(col, (chunk_rows, LANES))
        if own:
            a_s[here, :] = gates * (1.0 - score)
            sacc[:, here, :] = jnp.zeros((2, chunk_rows, LANES), F32)

        def piece(i, carry):
            r = pl.ds(pl.multiple_of(i * LANES, LANES), LANES)
            ra = pl.ds(pl.multiple_of(c * chunk_rows + i * LANES, LANES), LANES)
            for t in range(both // LANES):
                expert = t // tiles_e
                gate = gb[expert, ra, :]
                pre = pre_s[r, t * LANES : (t + 1) * LANES]
                up = pre_s[r, both + t * LANES : both + (t + 1) * LANES]
                q = q_s[r, t * LANES : (t + 1) * LANES]
                sig = 0.5 * jnp.tanh(0.5 * pre) + 0.5
                silu = pre * sig
                h = silu * up
                gq = gate * q
                hid[ra, t * LANES : (t + 1) * LANES] = (gate * h).astype(BF16)
                gu[ra, t * LANES : (t + 1) * LANES] = (gq * up * (sig + silu * (1.0 - sig))).astype(BF16)
                gu[ra, both + t * LANES : both + (t + 1) * LANES] = (gq * silu).astype(BF16)
                if own:
                    sacc[expert, ra, :] += h * q
            return carry

        lax.fori_loop(0, chunk_rows // LANES, piece, 0)
        return carry

    lax.fori_loop(0, rows // chunk_rows, chunk, 0)

    for copy in acc_copies:
        copy.wait()
    def weight_grad(i, grad):
        if not own:
            grad = grad + acc_s[i]
        acc_s[i] = grad
        if not last:
            pltpu.make_async_copy(acc_s.at[i], outs[0].at[i], sems.at[out_sem + i]).start()

    def from_tokens(i, carry):
        part = pl.ds(pl.multiple_of(i * both, LANES), both)
        weight_grad(i, mm(x_s[:, pl.ds(zcol, cols)], gu[:, part], TN))
        return carry

    lax.fori_loop(0, 2, from_tokens, 0)
    weight_grad(2, mm(o_s[:, pl.ds(zcol, cols)], hid[...], TN))
    if last:
        for i in range(2):
            for e in range(2):
                outs[i][e] = acc_s[i, :, e * ff : (e + 1) * ff].astype(BF16)
        for e in range(2):
            outs[2][e] = acc_s[2, :, e * ff : (e + 1) * ff].T.astype(BF16)

    if own:
        lane = lax.broadcasted_iota(jnp.int32, (rows, LANES), 1)
        term = jnp.zeros((rows, LANES), F32)
        shared = jnp.zeros((rows, LANES), F32)
        for j in range(2):
            sens = jnp.sum(sacc[j], axis=1, keepdims=True)
            term = term + jnp.where(lane == first_expert + j, sens, 0.0)
            shared = shared + gb[j] * sens
        grad = a_s[...] * (term - shared)
        high = grad.astype(BF16)
        low = (grad - high.astype(F32)).astype(BF16)
        gu[:, 2 * both : 2 * both + LANES] = high
        gu[:, 2 * both + LANES :] = low
        n_out = rp_out.shape[0]
        split = gu[:, 2 * both :]
        terms = mm(split, x_s[:, :width], TN)
        rp_out[...] = terms[:n_out] + terms[LANES : LANES + n_out]
    if not last:
        for i in range(3):
            pltpu.make_async_copy(acc_s.at[i], outs[0].at[i], sems.at[out_sem + i]).wait()


def expert_call(own, last, scal, blocks, wc, wd, acc, n_experts):
    tok = sum(b.shape[0] for b in blocks) // (2 * PLANE)
    units = tuple(b.shape[0] // (2 * tok) for b in blocks)
    both, width = wd.shape
    ff = both // 2
    cols = width // lax.axis_size("dp")
    rows = PLANE * tok
    anywhere = pl.BlockSpec(memory_space=pl.ANY)
    vmem = pl.BlockSpec(memory_space=pltpu.VMEM)
    args = [*blocks, wc, wd]
    if not own:
        args.append(acc)
    if last:
        out_shape = [jax.ShapeDtypeStruct((2, cols, ff), BF16)] * 2 + [jax.ShapeDtypeStruct((2, ff, cols), BF16)]
        out_specs = [vmem] * 3
    else:
        out_shape = [jax.ShapeDtypeStruct((3, cols, both), F32)]
        out_specs = [anywhere]
    if own:
        out_shape += [
            jax.ShapeDtypeStruct((rows, both), BF16),
            jax.ShapeDtypeStruct((rows, 2 * both + 2 * LANES), BF16),
            jax.ShapeDtypeStruct((n_experts, width), F32),
        ]
        out_specs += [vmem] * 3
    chunk = rows // 4
    scratch = [
        pltpu.VMEM((rows, width + LANES), BF16),
        pltpu.VMEM((rows, width), BF16),
        pltpu.VMEM((width, 2 * both + LANES), BF16),
        pltpu.VMEM((both, width), BF16),
        pltpu.VMEM((chunk, 2 * both + LANES), F32),
        pltpu.VMEM((chunk, both), F32),
        pltpu.VMEM((2, rows, LANES), F32),
        pltpu.VMEM((3, cols, both), F32),
    ]
    if own:
        scratch += [pltpu.VMEM((rows, LANES), F32), pltpu.VMEM((2, rows, LANES), F32)]
    else:
        scratch += [pltpu.VMEM((rows, both), BF16), pltpu.VMEM((rows, 2 * both), BF16)]
    scratch.append(pltpu.SemaphoreType.DMA((2 * PLANE + 7,)))
    aliases = {} if own or last else {1 + len(blocks) + 2: 0}
    flops = 2 * rows * width * both * 3 + 2 * rows * cols * both * 3
    return pl.pallas_call(
        functools.partial(expert_kernel, own, last, tok, width, ff, cols, units),
        grid_spec=pltpu.PrefetchScalarGridSpec(
            num_scalar_prefetch=1,
            grid=(),
            in_specs=[anywhere] * len(args),
            out_specs=out_specs,
            scratch_shapes=scratch,
        ),
        out_shape=out_shape,
        input_output_aliases=aliases,
        compiler_params=pltpu.CompilerParams(vmem_limit_bytes=58 * 1024 * 1024),
        cost_estimate=pl.CostEstimate(flops=flops, bytes_accessed=40_000_000, transcendentals=rows * both),
        name="experts_own" if own else "experts_last" if last else "experts_mid",
    )(scal, *args)


def flip(x, even, odd):
    groups = lax.axis_size("expert")
    return lax.ppermute(x, "expert", [(i, i ^ (odd if i % 2 else even)) for i in range(groups)])


def dense_body(tokens, expert_ids, router, w_gate, w_up, w_down, out_grad):
    tok, width = tokens.shape
    n_experts = router.shape[1]
    ff = w_gate.shape[2]
    n_dp = lax.axis_size("dp")
    me = lax.axis_index("expert")
    core = me % 2
    ladder = jnp.arange(LANES, dtype=jnp.int32)
    mask = jnp.any(expert_ids[:, :, None] == ladder[None, None, :], axis=1).astype(BF16)
    block = jnp.concatenate(
        [
            jnp.concatenate([tokens, mask], axis=1),
            jnp.concatenate([out_grad, jnp.zeros((tok, LANES), BF16)], axis=1),
        ],
        axis=0,
    )
    router_pad = jnp.pad(router, ((0, 0), (0, LANES - n_experts)))
    wc = jnp.concatenate([w_gate[0], w_gate[1], w_up[0], w_up[1], router_pad, router_pad], axis=1)
    wd = w_down.reshape(2 * ff, width)
    near_at = me ^ jnp.where(core == 0, 2, 4)
    other_at = me ^ jnp.where(core == 0, 5, 3)
    scal = jnp.stack(
        [me * 2, lax.axis_index("dp"), me, me ^ 1, near_at, near_at ^ 1, other_at, other_at ^ 1, me ^ 6, me ^ 7]
    ).astype(jnp.int32)
    ring = [(i, (i + 1) % n_dp) for i in range(n_dp)]

    def swap(b):
        return flip(b, 1, 1)

    def pair_of(b):
        return jnp.concatenate([b, swap(b)], axis=0)

    def over_link(b):
        return flip(b, 2, 4)

    def onward(near):
        return flip(near[: 2 * tok], 4, 2)

    def along(b):
        return lax.ppermute(b, "dp", ring)

    def hold(*values):
        return lax.optimization_barrier(values)

    def experts(g, acc, blocks):
        return expert_call(g == 0, g == n_dp - 1, scal, blocks, wc, wd, acc, n_experts)

    one = along(block)
    pair0 = pair_of(block)
    near0 = over_link(pair0)
    near0, one = hold(near0, one)
    diag0, other0, two, pair1 = onward(near0), swap(near0), along(one), pair_of(one)
    diag0, other0, one, pair1 = hold(diag0, other0, one, pair1)
    blocks0 = [pair0, near0, other0, diag0, swap(diag0)]

    near1, diag1 = over_link(pair1), flip(one, 6, 6)
    acc, hid, gu, rp = experts(0, None, blocks0)
    acc, hid, gu, rp, near1, diag1, two = hold(acc, hid, gu, rp, near1, diag1, two)
    blocks1 = [pair1, near1, swap(near1), diag1, swap(diag1)]

    pair2 = pair_of(two)
    near2, three = over_link(pair2), along(two)
    mixed_part = jnp.dot(hid, wd, preferred_element_type=F32).astype(BF16)
    mixed = lax.psum_scatter(mixed_part, "expert", scatter_dimension=0, tiled=True)
    token_part = mm(gu, wc, NT).astype(BF16)
    token_grad = lax.psum_scatter(token_part, "expert", scatter_dimension=0, tiled=True)
    rp = rp + swap(rp)
    acc, near2, three, rp, mixed_part, token_part = hold(acc, near2, three, rp, mixed_part, token_part)

    pair3 = pair_of(three)
    diag2, other2, near3 = onward(near2), swap(near2), over_link(pair3)
    (acc,) = experts(1, acc, blocks1)
    acc, diag2, other2, near3, rp = hold(acc, diag2, other2, near3, rp)
    blocks2 = [pair2, near2, other2, diag2, swap(diag2)]

    diag3, other3 = onward(near3), swap(near3)
    terms = [rp] + [flip(rp, k, k) for k in (2, 4, 6)]
    (acc,) = experts(2, acc, blocks2)
    acc, diag3, other3, *terms = hold(acc, diag3, other3, *terms)
    rp = (terms[0] + terms[1]) + (terms[2] + terms[3])
    terms = [rp] + [lax.ppermute(rp, "dp", [(i, i ^ k) for i in range(n_dp)]) for k in range(1, n_dp)]
    out = experts(3, acc, [pair3, near3, other3, diag3, swap(diag3)])
    out = hold(*out, *terms)
    terms = out[3:]
    rp = (terms[0] + terms[1]) + (terms[2] + terms[3])
    out = out[:3]
    return (mixed, token_grad, rp.T, *out)


def flat_rows(array):
    return array.reshape(array.shape[0], array.shape[1] * array.shape[2], array.shape[3])


def sparse_body(tokens, expert_ids, router, w_gate, w_up, w_down, out_grad):
    f32 = jnp.float32
    bf16 = jnp.bfloat16
    tok_dev, width = tokens.shape
    top = expert_ids.shape[1]
    n_experts = router.shape[1]
    local_experts = w_gate.shape[0]
    groups = lax.axis_size("expert")
    capacity = (tok_dev * top * 9 + 8 * n_experts - 1) // (8 * n_experts)
    n_assign = tok_dev * top
    flat_ids = expert_ids.reshape(-1)
    ladder = jnp.arange(n_experts, dtype=jnp.int32)
    onehot = (flat_ids[:, None] == ladder[None, :]).astype(jnp.int32)
    rank = jnp.sum((jnp.cumsum(onehot, axis=0) - onehot) * onehot, axis=1)
    owner = flat_ids // local_experts
    within = flat_ids % local_experts
    dest = (within * groups + owner) * capacity + rank
    slot_src = jnp.full((n_experts * capacity,), n_assign, jnp.int32)
    slot_src = slot_src.at[dest].set(jnp.arange(n_assign, dtype=jnp.int32))
    live = slot_src < n_assign
    slot_tok = jnp.where(live, slot_src // top, 0)
    logits = jnp.dot(tokens, router, preferred_element_type=f32)
    scores = jax.nn.sigmoid(logits)
    chosen = jnp.take_along_axis(scores, expert_ids, axis=1)
    total = jnp.sum(chosen, axis=1, keepdims=True)
    gates = chosen / total
    gate_slots = jnp.where(live, gates.reshape(-1)[jnp.minimum(slot_src, n_assign - 1)], 0.0)
    send = jnp.where(live[:, None], tokens[slot_tok], jnp.zeros((), bf16))
    send = send.reshape(local_experts, groups, capacity, width)
    piece = lax.all_to_all(send, "expert", split_axis=1, concat_axis=1, tiled=True)
    shape = piece.shape
    rows = flat_rows(piece)
    pre_gate = jnp.einsum("jrd,jdf->jrf", rows, w_gate, preferred_element_type=f32)
    pre_up = jnp.einsum("jrd,jdf->jrf", rows, w_up, preferred_element_type=f32)
    hidden = (pre_gate * jax.nn.sigmoid(pre_gate) * pre_up).astype(bf16)
    expert_out = jnp.einsum("jrf,jfd->jrd", hidden, w_down, preferred_element_type=f32).astype(bf16)
    hid_shape = (shape[0], shape[1], shape[2], hidden.shape[2])
    expert_out = expert_out.reshape(shape)
    hidden = hidden.reshape(hid_shape)
    results = (expert_out, hidden, piece, pre_gate.reshape(hid_shape), pre_up.reshape(hid_shape))
    expert_out = results[0]
    hidden = flat_rows(results[1])
    back = lax.all_to_all(expert_out, "expert", split_axis=1, concat_axis=1, tiled=True).reshape(
        n_experts * capacity, width
    )
    picked = back[dest].reshape(tok_dev, top, width)
    mixed = jnp.einsum("tk,tkd->td", gates, picked.astype(f32)).astype(bf16)
    gate_sens = jnp.einsum("tkd,td->tk", picked, out_grad, preferred_element_type=f32)
    grad_rows = (gate_slots[:, None] * out_grad[slot_tok].astype(f32)).astype(bf16)
    grad_send = jnp.where(live[:, None], grad_rows, jnp.zeros((), bf16))
    grad_send = grad_send.reshape(local_experts, groups, capacity, width)
    grad_in4 = lax.all_to_all(grad_send, "expert", split_axis=1, concat_axis=1, tiled=True)
    grad_in = flat_rows(grad_in4)
    pre_gate = flat_rows(results[3])
    pre_up = flat_rows(results[4])
    hidden_grad = jnp.einsum("jrd,jfd->jrf", grad_in, w_down, preferred_element_type=f32)
    sig = jax.nn.sigmoid(pre_gate)
    silu_val = pre_gate * sig
    gate_term = (hidden_grad * pre_up * sig * (1.0 + pre_gate * (1.0 - sig))).astype(bf16)
    up_term = (hidden_grad * silu_val).astype(bf16)
    input_grad = (
        jnp.einsum("jrf,jdf->jrd", gate_term, w_gate, preferred_element_type=f32)
        + jnp.einsum("jrf,jdf->jrd", up_term, w_up, preferred_element_type=f32)
    ).astype(bf16)
    input_grad = input_grad.reshape(grad_in4.shape)
    returned = lax.all_to_all(
        input_grad, "expert", split_axis=1, concat_axis=1, tiled=True
    ).reshape(n_experts * capacity, width)
    moe_grad = jnp.sum(returned[dest].reshape(tok_dev, top, width).astype(f32), axis=1)
    chosen_grad = (gate_sens - jnp.sum(gate_sens * gates, axis=1, keepdims=True)) / total
    sel_grad = chosen_grad * chosen * (1.0 - chosen)
    pick = (expert_ids[:, :, None] == ladder[None, None, :]).astype(f32)
    logit_grad = jnp.einsum("tk,tke->te", sel_grad, pick).astype(bf16)
    token_grad = (moe_grad + jnp.dot(logit_grad, router.T, preferred_element_type=f32)).astype(bf16)
    router_grad = lax.psum(
        jnp.dot(tokens.T, logit_grad, preferred_element_type=f32), ("expert", "dp")
    )
    hidden_width = hidden.shape[2]
    arrived4 = results[2]
    columns = (
        lax.all_to_all(arrived4, "dp", split_axis=3, concat_axis=1, tiled=True),
        lax.all_to_all(grad_in4, "dp", split_axis=3, concat_axis=1, tiled=True),
    )
    hid_shape = (local_experts, groups, capacity, hidden_width)
    hiddens = (
        lax.all_gather(gate_term.reshape(hid_shape), "dp", axis=1, tiled=True),
        lax.all_gather(up_term.reshape(hid_shape), "dp", axis=1, tiled=True),
        lax.all_gather(results[1], "dp", axis=1, tiled=True),
    )
    x_cols = flat_rows(columns[0])
    g_cols = flat_rows(columns[1])
    gate_grad = jnp.einsum(
        "jrd,jrf->jdf", x_cols, flat_rows(hiddens[0]), preferred_element_type=f32
    ).astype(bf16)
    up_grad = jnp.einsum(
        "jrd,jrf->jdf", x_cols, flat_rows(hiddens[1]), preferred_element_type=f32
    ).astype(bf16)
    down_grad = jnp.einsum(
        "jrf,jrd->jfd", flat_rows(hiddens[2]), g_cols, preferred_element_type=f32
    ).astype(bf16)
    return (mixed, token_grad, router_grad, gate_grad, up_grad, down_grad)


def body(*args):
    plane = lax.axis_size("expert") == 8 and args[3].shape[0] == 2
    line = lax.axis_size("dp")
    return (dense_body if plane and line == 4 else sparse_body)(*args)


def solution(mesh):
    placed = (
        P(("expert", "dp"), None),
        P(("expert", "dp"), None),
        P(),
        P("expert", None, None),
        P("expert", None, None),
        P("expert", None, None),
        P(("expert", "dp"), None),
    )
    return jax.shard_map(
        body,
        mesh=mesh,
        in_specs=placed,
        out_specs=(
            P(("expert", "dp"), None),
            P(("expert", "dp"), None),
            P(),
            P("expert", "dp", None),
            P("expert", "dp", None),
            P("expert", None, "dp"),
        ),
        check_vma=False,
    )
```

```python
import functools

import jax
import jax.numpy as jnp
from jax import lax
from jax.experimental import pallas as pl
from jax.experimental.pallas import tpu as pltpu
from jax.sharding import PartitionSpec as P

F32 = jnp.float32
BF16 = jnp.bfloat16
LANES = 128
PLANE = 8


def mm(a, b, contract):
    return lax.dot_general(a, b, (contract, ((), ())), preferred_element_type=F32)


NN = ((1,), (0,))
NT = ((1,), (1,))
TN = ((0,), (0,))


def expert_kernel(own, last, tok, width, ff, cols, units, *refs):
    refs = list(refs)
    scal = refs.pop(0)
    blocks = [refs.pop(0) for _ in units]
    wc, wd = refs.pop(0), refs.pop(0)
    acc_in = None if own else refs.pop(0)
    outs = [refs.pop(0) for _ in range(3 if last else 1)]
    if own:
        hid, gu, rp_out = (refs.pop(0) for _ in range(3))
    x_s, o_s, wc_s, wd_s, pre_s, q_s, gb, acc_s = (refs.pop(0) for _ in range(8))
    if own:
        a_s, sacc = refs.pop(0), refs.pop(0)
    else:
        hid, gu = refs.pop(0), refs.pop(0)
    sems = refs.pop(0)
    rows = PLANE * tok
    both = 2 * ff
    chunk_rows = pre_s.shape[0]
    first_expert = scal[0]
    zcol = pl.multiple_of(scal[1] * cols, LANES)
    tiles_e = ff // LANES

    taken = iter(range(64))
    x_copies, o_copies = [], []
    place = 2
    for ref, count in zip(blocks, units):
        for u in range(count):
            at = pl.ds(pl.multiple_of(scal[place] * tok, tok), tok)
            place += 1
            base = 2 * tok * u
            x_copies.append(
                pltpu.make_async_copy(ref.at[pl.ds(base, tok), :], x_s.at[at, :], sems.at[next(taken)])
            )
            o_copies.append(
                pltpu.make_async_copy(
                    ref.at[pl.ds(base + tok, tok), pl.ds(0, width)], o_s.at[at, :], sems.at[next(taken)]
                )
            )

    def part(src, dst, lo, size):
        return pltpu.make_async_copy(
            src.at[:, pl.ds(lo, size)], dst.at[:, pl.ds(lo, size)], sems.at[next(taken)]
        )

    gate_copy = part(wc, wc_s, 0, both)
    up_copy = part(wc, wc_s, both, both + LANES)
    wd_copy = pltpu.make_async_copy(wd, wd_s, sems.at[next(taken)])
    acc_copies = []
    if not own:
        acc_copies = [pltpu.make_async_copy(acc_in, acc_s, sems.at[next(taken)])]
    for copy in [*o_copies, wd_copy, *x_copies, gate_copy, up_copy, *acc_copies]:
        copy.start()
    out_sem = next(taken)
    for copy in [*o_copies, wd_copy]:
        copy.wait()

    def back(c, carry):
        here = pl.ds(pl.multiple_of(c * chunk_rows, chunk_rows), chunk_rows)
        q_s[here, :] = mm(o_s[here, :], wd_s[...], NT)
        return carry

    lax.fori_loop(0, rows // chunk_rows, back, 0)
    for copy in [*x_copies, gate_copy, up_copy]:
        copy.wait()

    lane = lax.broadcasted_iota(jnp.int32, (chunk_rows, LANES), 1)

    def chunk(c, carry):
        here = pl.ds(pl.multiple_of(c * chunk_rows, chunk_rows), chunk_rows)
        pre_s[...] = mm(x_s[here, :width], wc_s[...], NN)
        score = jax.nn.sigmoid(pre_s[:, 2 * both :])
        chosen = score * x_s[here, width:].astype(F32)
        gates = chosen / jnp.sum(chosen, axis=1, keepdims=True)
        for j in range(2):
            col = jnp.sum(jnp.where(lane == first_expert + j, gates, 0.0), axis=1, keepdims=True)
            gb[j, here, :] = jnp.broadcast_to(col, (chunk_rows, LANES))
        if own:
            a_s[here, :] = gates * (1.0 - score)
            sacc[:, here, :] = jnp.zeros((2, chunk_rows, LANES), F32)

        def piece(i, carry):
            r = pl.ds(pl.multiple_of(i * LANES, LANES), LANES)
            ra = pl.ds(pl.multiple_of(c * chunk_rows + i * LANES, LANES), LANES)
            for t in range(both // LANES):
                expert = t // tiles_e
                gate = gb[expert, ra, :]
                pre = pre_s[r, t * LANES : (t + 1) * LANES]
                up = pre_s[r, both + t * LANES : both + (t + 1) * LANES]
                q = q_s[ra, t * LANES : (t + 1) * LANES]
                sig = 0.5 * jnp.tanh(0.5 * pre) + 0.5
                silu = pre * sig
                h = silu * up
                gq = gate * q
                hid[ra, t * LANES : (t + 1) * LANES] = (gate * h).astype(BF16)
                gu[ra, t * LANES : (t + 1) * LANES] = (gq * up * (sig + silu * (1.0 - sig))).astype(BF16)
                gu[ra, both + t * LANES : both + (t + 1) * LANES] = (gq * silu).astype(BF16)
                if own:
                    sacc[expert, ra, :] += h * q
            return carry

        lax.fori_loop(0, chunk_rows // LANES, piece, 0)
        return carry

    lax.fori_loop(0, rows // chunk_rows, chunk, 0)

    for copy in acc_copies:
        copy.wait()
    def weight_grad(i, grad):
        if not own:
            grad = grad + acc_s[i]
        acc_s[i] = grad
        if not last:
            pltpu.make_async_copy(acc_s.at[i], outs[0].at[i], sems.at[out_sem + i]).start()

    def from_tokens(i, carry):
        part = pl.ds(pl.multiple_of(i * both, LANES), both)
        weight_grad(i, mm(x_s[:, pl.ds(zcol, cols)], gu[:, part], TN))
        return carry

    lax.fori_loop(0, 2, from_tokens, 0)
    weight_grad(2, mm(o_s[:, pl.ds(zcol, cols)], hid[...], TN))
    if last:
        for i in range(2):
            for e in range(2):
                outs[i][e] = acc_s[i, :, e * ff : (e + 1) * ff].astype(BF16)
        for e in range(2):
            outs[2][e] = acc_s[2, :, e * ff : (e + 1) * ff].T.astype(BF16)

    if own:
        lane = lax.broadcasted_iota(jnp.int32, (rows, LANES), 1)
        term = jnp.zeros((rows, LANES), F32)
        shared = jnp.zeros((rows, LANES), F32)
        for j in range(2):
            sens = jnp.sum(sacc[j], axis=1, keepdims=True)
            term = term + jnp.where(lane == first_expert + j, sens, 0.0)
            shared = shared + gb[j] * sens
        grad = a_s[...] * (term - shared)
        high = grad.astype(BF16)
        low = (grad - high.astype(F32)).astype(BF16)
        gu[:, 2 * both : 2 * both + LANES] = high
        gu[:, 2 * both + LANES :] = low
        n_out = rp_out.shape[0]
        split = gu[:, 2 * both :]
        terms = mm(split, x_s[:, :width], TN)
        rp_out[...] = terms[:n_out] + terms[LANES : LANES + n_out]
    if not last:
        for i in range(3):
            pltpu.make_async_copy(acc_s.at[i], outs[0].at[i], sems.at[out_sem + i]).wait()


def expert_call(own, last, scal, blocks, wc, wd, acc, n_experts):
    tok = sum(b.shape[0] for b in blocks) // (2 * PLANE)
    units = tuple(b.shape[0] // (2 * tok) for b in blocks)
    both, width = wd.shape
    ff = both // 2
    cols = width // lax.axis_size("dp")
    rows = PLANE * tok
    anywhere = pl.BlockSpec(memory_space=pl.ANY)
    vmem = pl.BlockSpec(memory_space=pltpu.VMEM)
    args = [*blocks, wc, wd]
    if not own:
        args.append(acc)
    if last:
        out_shape = [jax.ShapeDtypeStruct((2, cols, ff), BF16)] * 2 + [jax.ShapeDtypeStruct((2, ff, cols), BF16)]
        out_specs = [vmem] * 3
    else:
        out_shape = [jax.ShapeDtypeStruct((3, cols, both), F32)]
        out_specs = [anywhere]
    if own:
        out_shape += [
            jax.ShapeDtypeStruct((rows, both), BF16),
            jax.ShapeDtypeStruct((rows, 2 * both + 2 * LANES), BF16),
            jax.ShapeDtypeStruct((n_experts, width), F32),
        ]
        out_specs += [vmem] * 3
    chunk = rows // 4
    scratch = [
        pltpu.VMEM((rows, width + LANES), BF16),
        pltpu.VMEM((rows, width), BF16),
        pltpu.VMEM((width, 2 * both + LANES), BF16),
        pltpu.VMEM((both, width), BF16),
        pltpu.VMEM((chunk, 2 * both + LANES), F32),
        pltpu.VMEM((rows, both), F32),
        pltpu.VMEM((2, rows, LANES), F32),
        pltpu.VMEM((3, cols, both), F32),
    ]
    if own:
        scratch += [pltpu.VMEM((rows, LANES), F32), pltpu.VMEM((2, rows, LANES), F32)]
    else:
        scratch += [pltpu.VMEM((rows, both), BF16), pltpu.VMEM((rows, 2 * both), BF16)]
    scratch.append(pltpu.SemaphoreType.DMA((2 * PLANE + 7,)))
    aliases = {} if own or last else {1 + len(blocks) + 2: 0}
    flops = 2 * rows * width * both * 3 + 2 * rows * cols * both * 3
    return pl.pallas_call(
        functools.partial(expert_kernel, own, last, tok, width, ff, cols, units),
        grid_spec=pltpu.PrefetchScalarGridSpec(
            num_scalar_prefetch=1,
            grid=(),
            in_specs=[anywhere] * len(args),
            out_specs=out_specs,
            scratch_shapes=scratch,
        ),
        out_shape=out_shape,
        input_output_aliases=aliases,
        compiler_params=pltpu.CompilerParams(vmem_limit_bytes=58 * 1024 * 1024),
        cost_estimate=pl.CostEstimate(flops=flops, bytes_accessed=40_000_000, transcendentals=rows * both),
        name="experts_own" if own else "experts_last" if last else "experts_mid",
    )(scal, *args)


def flip(x, even, odd):
    groups = lax.axis_size("expert")
    return lax.ppermute(x, "expert", [(i, i ^ (odd if i % 2 else even)) for i in range(groups)])


def dense_body(tokens, expert_ids, router, w_gate, w_up, w_down, out_grad):
    tok, width = tokens.shape
    n_experts = router.shape[1]
    ff = w_gate.shape[2]
    n_dp = lax.axis_size("dp")
    me = lax.axis_index("expert")
    core = me % 2
    ladder = jnp.arange(LANES, dtype=jnp.int32)
    mask = jnp.any(expert_ids[:, :, None] == ladder[None, None, :], axis=1).astype(BF16)
    block = jnp.concatenate(
        [
            jnp.concatenate([tokens, mask], axis=1),
            jnp.concatenate([out_grad, jnp.zeros((tok, LANES), BF16)], axis=1),
        ],
        axis=0,
    )
    router_pad = jnp.pad(router, ((0, 0), (0, LANES - n_experts)))
    wc = jnp.concatenate([w_gate[0], w_gate[1], w_up[0], w_up[1], router_pad, router_pad], axis=1)
    wd = w_down.reshape(2 * ff, width)
    near_at = jnp.where(core == 0, 1, 2)
    scal = jnp.stack(
        [me * 2, lax.axis_index("dp"), 0, 4, near_at, near_at + 4, 7 - near_at, 3 - near_at, 3, 7]
    ).astype(jnp.int32)
    ring = [(i, (i + 1) % n_dp) for i in range(n_dp)]

    def swap(b):
        return flip(b, 1, 1)

    def pair_of(b):
        return jnp.concatenate([b, swap(b)], axis=0)

    def over_link(b):
        return flip(b, 2, 4)

    def onward(near):
        return flip(near[: 2 * tok], 4, 2)

    def along(b):
        return lax.ppermute(b, "dp", ring)

    def hold(*values):
        return lax.optimization_barrier(values)

    def experts(g, acc, blocks):
        return expert_call(g == 0, g == n_dp - 1, scal, blocks, wc, wd, acc, n_experts)

    def rows_of(x, j):
        return x[j * tok : (j + 1) * tok].astype(F32)

    def core_sums(low, other):
        return [rows_of(low, 0) + rows_of(other, 0)] + [
            (rows_of(low, j) + rows_of(other, j)).astype(BF16) for j in range(1, 4)
        ]

    def plane_total(mine, arrived):
        for a in arrived:
            mine = mine + a.astype(F32)
        return mine.astype(BF16)

    one = along(block)
    pair0 = pair_of(block)
    near0 = over_link(pair0)
    near0, one, wc = hold(near0, one, wc)
    diag0, other0, two, pair1 = onward(near0), swap(near0), along(one), pair_of(one)
    diag0, other0, one, pair1 = hold(diag0, other0, one, pair1)
    blocks0 = [pair0, near0, other0, diag0, swap(diag0)]

    near1, diag1 = over_link(pair1), flip(one, 6, 6)
    acc, hid, gu, rp = experts(0, None, blocks0)
    acc, hid, gu, rp, near1, diag1, two = hold(acc, hid, gu, rp, near1, diag1, two)
    blocks1 = [pair1, near1, swap(near1), diag1, swap(diag1)]

    pair2, hid, gu = hold(pair_of(two), hid, gu)
    near2, three = over_link(pair2), along(two)
    rp = rp + swap(rp)
    rp_z = lax.ppermute(rp, "dp", [(i, i ^ 1) for i in range(n_dp)])
    rows = 4 * tok
    mixed_high = jnp.dot(hid[rows:], wd, preferred_element_type=F32).astype(BF16)
    mixed_low = jnp.dot(hid[:rows], wd, preferred_element_type=F32).astype(BF16)
    mixed_other = swap(mixed_high)
    token_high = mm(gu[rows:], wc, NT).astype(BF16)
    token_low = mm(gu[:rows], wc, NT).astype(BF16)
    acc, near2, three, rp, rp_z, mixed_low, mixed_other, token_low, token_high = hold(
        acc, near2, three, rp, rp_z, mixed_low, mixed_other, token_low, token_high
    )

    rp = rp + rp_z
    pair3 = pair_of(three)
    diag2, other2, near3 = onward(near2), swap(near2), over_link(pair3)
    token_other = swap(token_high)
    rp_z = lax.ppermute(rp, "dp", [(i, i ^ 2) for i in range(n_dp)])
    (acc,) = experts(1, acc, blocks1)
    acc, diag2, other2, near3, rp, rp_z, token_other, token_low, mixed_low, mixed_other = hold(
        acc, diag2, other2, near3, rp, rp_z, token_other, token_low, mixed_low, mixed_other
    )
    blocks2 = [pair2, near2, other2, diag2, swap(diag2)]

    rp = rp + rp_z
    mixed_sums = core_sums(mixed_low, mixed_other)
    diag3, other3 = onward(near3), swap(near3)
    mixed_x, mixed_y = flip(mixed_sums[1], 2, 2), flip(mixed_sums[2], 4, 4)
    rp_x = flip(rp, 2, 2)
    (acc,) = experts(2, acc, blocks2)
    acc, diag3, other3, mixed_x, mixed_y, rp, rp_x, token_low, token_other, *mixed_sums = hold(
        acc, diag3, other3, mixed_x, mixed_y, rp, rp_x, token_low, token_other, *mixed_sums
    )

    rp = rp + rp_x
    token_sums = core_sums(token_low, token_other)
    mixed_d = flip(mixed_sums[3], 6, 6)
    token_parts = [flip(t, k, k) for t, k in zip(token_sums[1:], (2, 4, 6))]
    rp_y = flip(rp, 4, 4)
    out = experts(3, acc, [pair3, near3, other3, diag3, swap(diag3)])
    *out, mixed_d, rp_y, token_x, token_y, token_d = hold(*out, mixed_d, rp_y, *token_parts)
    mixed = plane_total(mixed_sums[0], (mixed_x, mixed_y, mixed_d))
    token_grad = plane_total(token_sums[0], (token_x, token_y, token_d))
    rp = rp + rp_y
    return (mixed, token_grad, rp.T, *out)


def flat_rows(array):
    return array.reshape(array.shape[0], array.shape[1] * array.shape[2], array.shape[3])


def sparse_body(tokens, expert_ids, router, w_gate, w_up, w_down, out_grad):
    f32 = jnp.float32
    bf16 = jnp.bfloat16
    tok_dev, width = tokens.shape
    top = expert_ids.shape[1]
    n_experts = router.shape[1]
    local_experts = w_gate.shape[0]
    groups = lax.axis_size("expert")
    capacity = (tok_dev * top * 9 + 8 * n_experts - 1) // (8 * n_experts)
    n_assign = tok_dev * top
    flat_ids = expert_ids.reshape(-1)
    ladder = jnp.arange(n_experts, dtype=jnp.int32)
    onehot = (flat_ids[:, None] == ladder[None, :]).astype(jnp.int32)
    rank = jnp.sum((jnp.cumsum(onehot, axis=0) - onehot) * onehot, axis=1)
    owner = flat_ids // local_experts
    within = flat_ids % local_experts
    dest = (within * groups + owner) * capacity + rank
    slot_src = jnp.full((n_experts * capacity,), n_assign, jnp.int32)
    slot_src = slot_src.at[dest].set(jnp.arange(n_assign, dtype=jnp.int32))
    live = slot_src < n_assign
    slot_tok = jnp.where(live, slot_src // top, 0)
    logits = jnp.dot(tokens, router, preferred_element_type=f32)
    scores = jax.nn.sigmoid(logits)
    chosen = jnp.take_along_axis(scores, expert_ids, axis=1)
    total = jnp.sum(chosen, axis=1, keepdims=True)
    gates = chosen / total
    gate_slots = jnp.where(live, gates.reshape(-1)[jnp.minimum(slot_src, n_assign - 1)], 0.0)
    send = jnp.where(live[:, None], tokens[slot_tok], jnp.zeros((), bf16))
    send = send.reshape(local_experts, groups, capacity, width)
    piece = lax.all_to_all(send, "expert", split_axis=1, concat_axis=1, tiled=True)
    shape = piece.shape
    rows = flat_rows(piece)
    pre_gate = jnp.einsum("jrd,jdf->jrf", rows, w_gate, preferred_element_type=f32)
    pre_up = jnp.einsum("jrd,jdf->jrf", rows, w_up, preferred_element_type=f32)
    hidden = (pre_gate * jax.nn.sigmoid(pre_gate) * pre_up).astype(bf16)
    expert_out = jnp.einsum("jrf,jfd->jrd", hidden, w_down, preferred_element_type=f32).astype(bf16)
    hid_shape = (shape[0], shape[1], shape[2], hidden.shape[2])
    expert_out = expert_out.reshape(shape)
    hidden = hidden.reshape(hid_shape)
    results = (expert_out, hidden, piece, pre_gate.reshape(hid_shape), pre_up.reshape(hid_shape))
    expert_out = results[0]
    hidden = flat_rows(results[1])
    back = lax.all_to_all(expert_out, "expert", split_axis=1, concat_axis=1, tiled=True).reshape(
        n_experts * capacity, width
    )
    picked = back[dest].reshape(tok_dev, top, width)
    mixed = jnp.einsum("tk,tkd->td", gates, picked.astype(f32)).astype(bf16)
    gate_sens = jnp.einsum("tkd,td->tk", picked, out_grad, preferred_element_type=f32)
    grad_rows = (gate_slots[:, None] * out_grad[slot_tok].astype(f32)).astype(bf16)
    grad_send = jnp.where(live[:, None], grad_rows, jnp.zeros((), bf16))
    grad_send = grad_send.reshape(local_experts, groups, capacity, width)
    grad_in4 = lax.all_to_all(grad_send, "expert", split_axis=1, concat_axis=1, tiled=True)
    grad_in = flat_rows(grad_in4)
    pre_gate = flat_rows(results[3])
    pre_up = flat_rows(results[4])
    hidden_grad = jnp.einsum("jrd,jfd->jrf", grad_in, w_down, preferred_element_type=f32)
    sig = jax.nn.sigmoid(pre_gate)
    silu_val = pre_gate * sig
    gate_term = (hidden_grad * pre_up * sig * (1.0 + pre_gate * (1.0 - sig))).astype(bf16)
    up_term = (hidden_grad * silu_val).astype(bf16)
    input_grad = (
        jnp.einsum("jrf,jdf->jrd", gate_term, w_gate, preferred_element_type=f32)
        + jnp.einsum("jrf,jdf->jrd", up_term, w_up, preferred_element_type=f32)
    ).astype(bf16)
    input_grad = input_grad.reshape(grad_in4.shape)
    returned = lax.all_to_all(
        input_grad, "expert", split_axis=1, concat_axis=1, tiled=True
    ).reshape(n_experts * capacity, width)
    moe_grad = jnp.sum(returned[dest].reshape(tok_dev, top, width).astype(f32), axis=1)
    chosen_grad = (gate_sens - jnp.sum(gate_sens * gates, axis=1, keepdims=True)) / total
    sel_grad = chosen_grad * chosen * (1.0 - chosen)
    pick = (expert_ids[:, :, None] == ladder[None, None, :]).astype(f32)
    logit_grad = jnp.einsum("tk,tke->te", sel_grad, pick).astype(bf16)
    token_grad = (moe_grad + jnp.dot(logit_grad, router.T, preferred_element_type=f32)).astype(bf16)
    router_grad = lax.psum(
        jnp.dot(tokens.T, logit_grad, preferred_element_type=f32), ("expert", "dp")
    )
    hidden_width = hidden.shape[2]
    arrived4 = results[2]
    columns = (
        lax.all_to_all(arrived4, "dp", split_axis=3, concat_axis=1, tiled=True),
        lax.all_to_all(grad_in4, "dp", split_axis=3, concat_axis=1, tiled=True),
    )
    hid_shape = (local_experts, groups, capacity, hidden_width)
    hiddens = (
        lax.all_gather(gate_term.reshape(hid_shape), "dp", axis=1, tiled=True),
        lax.all_gather(up_term.reshape(hid_shape), "dp", axis=1, tiled=True),
        lax.all_gather(results[1], "dp", axis=1, tiled=True),
    )
    x_cols = flat_rows(columns[0])
    g_cols = flat_rows(columns[1])
    gate_grad = jnp.einsum(
        "jrd,jrf->jdf", x_cols, flat_rows(hiddens[0]), preferred_element_type=f32
    ).astype(bf16)
    up_grad = jnp.einsum(
        "jrd,jrf->jdf", x_cols, flat_rows(hiddens[1]), preferred_element_type=f32
    ).astype(bf16)
    down_grad = jnp.einsum(
        "jrf,jrd->jfd", flat_rows(hiddens[2]), g_cols, preferred_element_type=f32
    ).astype(bf16)
    return (mixed, token_grad, router_grad, gate_grad, up_grad, down_grad)


def body(*args):
    plane = lax.axis_size("expert") == 8 and args[3].shape[0] == 2
    line = lax.axis_size("dp")
    return (dense_body if plane and line == 4 else sparse_body)(*args)


def solution(mesh):
    placed = (
        P(("expert", "dp"), None),
        P(("expert", "dp"), None),
        P(),
        P("expert", None, None),
        P("expert", None, None),
        P("expert", None, None),
        P(("expert", "dp"), None),
    )
    return jax.shard_map(
        body,
        mesh=mesh,
        in_specs=placed,
        out_specs=(
            P(("expert", "dp"), None),
            P(("expert", "dp"), None),
            P(),
            P("expert", "dp", None),
            P("expert", "dp", None),
            P("expert", None, "dp"),
        ),
        check_vma=False,
    )
```

```python
import functools

import jax
import jax.numpy as jnp
from jax import lax
from jax.experimental import pallas as pl
from jax.experimental.pallas import tpu as pltpu
from jax.sharding import PartitionSpec as P

F32 = jnp.float32
BF16 = jnp.bfloat16
LANES = 128
PLANE = 8


def mm(a, b, contract):
    return lax.dot_general(a, b, (contract, ((), ())), preferred_element_type=F32)


NN = ((1,), (0,))
NT = ((1,), (1,))
TN = ((0,), (0,))


def expert_kernel(own, last, tok, width, ff, cols, units, *refs):
    refs = list(refs)
    scal = refs.pop(0)
    blocks = [refs.pop(0) for _ in units]
    wc, wd = refs.pop(0), refs.pop(0)
    acc_in = None if own else refs.pop(0)
    outs = [refs.pop(0) for _ in range(3 if last else 1)]
    if own:
        part_outs, rp_out = [refs.pop(0) for _ in range(4)], refs.pop(0)
    x_s, o_s, wc_s, wd_s, pre_s, q_s, gb, acc_s = (refs.pop(0) for _ in range(8))
    if own:
        a_s, sacc = refs.pop(0), refs.pop(0)
    hid, gu = refs.pop(0), refs.pop(0)
    sems = refs.pop(0)
    rows = PLANE * tok
    both = 2 * ff
    chunk_rows = pre_s.shape[0]
    first_expert = scal[0]
    zcol = pl.multiple_of(scal[1] * cols, LANES)
    tiles_e = ff // LANES

    taken = iter(range(64))
    x_copies, o_copies = [], []
    place = 2
    for ref, count in zip(blocks, units):
        for u in range(count):
            at = pl.ds(pl.multiple_of(scal[place] * tok, tok), tok)
            place += 1
            base = 2 * tok * u
            x_copies.append(
                pltpu.make_async_copy(ref.at[pl.ds(base, tok), :], x_s.at[at, :], sems.at[next(taken)])
            )
            o_copies.append(
                pltpu.make_async_copy(
                    ref.at[pl.ds(base + tok, tok), pl.ds(0, width)], o_s.at[at, :], sems.at[next(taken)]
                )
            )

    def part(src, dst, lo, size):
        return pltpu.make_async_copy(
            src.at[:, pl.ds(lo, size)], dst.at[:, pl.ds(lo, size)], sems.at[next(taken)]
        )

    gate_copy = part(wc, wc_s, 0, both)
    up_copy = part(wc, wc_s, both, both + LANES)
    wd_copy = pltpu.make_async_copy(wd, wd_s, sems.at[next(taken)])
    acc_copies = []
    if not own:
        acc_copies = [pltpu.make_async_copy(acc_in, acc_s, sems.at[next(taken)])]
    for copy in [*o_copies, wd_copy, *x_copies, gate_copy, up_copy, *acc_copies]:
        copy.start()
    out_sem = next(taken)
    for copy in [*o_copies, wd_copy]:
        copy.wait()

    def back(c, carry):
        here = pl.ds(pl.multiple_of(c * chunk_rows, chunk_rows), chunk_rows)
        q_s[here, :] = mm(o_s[here, :], wd_s[...], NT)
        return carry

    lax.fori_loop(0, rows // chunk_rows, back, 0)
    for copy in [*x_copies, gate_copy, up_copy]:
        copy.wait()

    lane = lax.broadcasted_iota(jnp.int32, (chunk_rows, LANES), 1)

    def chunk(c, carry):
        here = pl.ds(pl.multiple_of(c * chunk_rows, chunk_rows), chunk_rows)
        pre_s[...] = mm(x_s[here, :width], wc_s[...], NN)
        score = jax.nn.sigmoid(pre_s[:, 2 * both :])
        chosen = score * x_s[here, width:].astype(F32)
        gates = chosen / jnp.sum(chosen, axis=1, keepdims=True)
        for j in range(2):
            col = jnp.sum(jnp.where(lane == first_expert + j, gates, 0.0), axis=1, keepdims=True)
            gb[j, here, :] = jnp.broadcast_to(col, (chunk_rows, LANES))
        if own:
            a_s[here, :] = gates * (1.0 - score)
            sacc[:, here, :] = jnp.zeros((2, chunk_rows, LANES), F32)

        def piece(i, carry):
            r = pl.ds(pl.multiple_of(i * LANES, LANES), LANES)
            ra = pl.ds(pl.multiple_of(c * chunk_rows + i * LANES, LANES), LANES)
            for t in range(both // LANES):
                expert = t // tiles_e
                gate = gb[expert, ra, :]
                pre = pre_s[r, t * LANES : (t + 1) * LANES]
                up = pre_s[r, both + t * LANES : both + (t + 1) * LANES]
                q = q_s[ra, t * LANES : (t + 1) * LANES]
                sig = 0.5 * jnp.tanh(0.5 * pre) + 0.5
                silu = pre * sig
                h = silu * up
                gq = gate * q
                hid[ra, t * LANES : (t + 1) * LANES] = (gate * h).astype(BF16)
                gu[ra, t * LANES : (t + 1) * LANES] = (gq * up * (sig + silu * (1.0 - sig))).astype(BF16)
                gu[ra, both + t * LANES : both + (t + 1) * LANES] = (gq * silu).astype(BF16)
                if own:
                    sacc[expert, ra, :] += h * q
            return carry

        lax.fori_loop(0, chunk_rows // LANES, piece, 0)
        return carry

    lax.fori_loop(0, rows // chunk_rows, chunk, 0)

    for copy in acc_copies:
        copy.wait()
    def weight_grad(i, grad):
        if not own:
            grad = grad + acc_s[i]
        acc_s[i] = grad
        if not last:
            pltpu.make_async_copy(acc_s.at[i], outs[0].at[i], sems.at[out_sem + i]).start()

    def from_tokens(i, carry):
        part = pl.ds(pl.multiple_of(i * both, LANES), both)
        weight_grad(i, mm(x_s[:, pl.ds(zcol, cols)], gu[:, part], TN))
        return carry

    lax.fori_loop(0, 2, from_tokens, 0)
    weight_grad(2, mm(o_s[:, pl.ds(zcol, cols)], hid[...], TN))
    if last:
        for i in range(2):
            for e in range(2):
                outs[i][e] = acc_s[i, :, e * ff : (e + 1) * ff].astype(BF16)
        for e in range(2):
            outs[2][e] = acc_s[2, :, e * ff : (e + 1) * ff].T.astype(BF16)

    if own:
        lane = lax.broadcasted_iota(jnp.int32, (rows, LANES), 1)
        term = jnp.zeros((rows, LANES), F32)
        shared = jnp.zeros((rows, LANES), F32)
        for j in range(2):
            sens = jnp.sum(sacc[j], axis=1, keepdims=True)
            term = term + jnp.where(lane == first_expert + j, sens, 0.0)
            shared = shared + gb[j] * sens
        grad = a_s[...] * (term - shared)
        high = grad.astype(BF16)
        low = (grad - high.astype(F32)).astype(BF16)
        gu[:, 2 * both : 2 * both + LANES] = high
        gu[:, 2 * both + LANES :] = low
        n_out = rp_out.shape[0]
        split = gu[:, 2 * both :]
        terms = mm(split, x_s[:, :width], TN)
        rp_out[...] = terms[:n_out] + terms[LANES : LANES + n_out]

        def mix(c, carry):
            here = pl.ds(pl.multiple_of(c * chunk_rows, chunk_rows), chunk_rows)
            o_s[here, :] = mm(hid[here, :], wd_s[...], NN).astype(BF16)
            return carry

        def token(c, carry):
            here = pl.ds(pl.multiple_of(c * chunk_rows, chunk_rows), chunk_rows)
            grad = mm(gu[here, : 2 * both + LANES], wc_s[...], NT)
            x_s[here, :width] = (grad + mm(gu[here, 2 * both + LANES :], wc_s[:, 2 * both :], NT)).astype(BF16)
            return carry

        finals = []
        for place, (step, kept) in enumerate(((mix, o_s), (token, x_s))):
            lax.fori_loop(0, rows // chunk_rows, step, 0)
            for j in range(2):
                half = pl.ds(j * rows // 2, rows // 2)
                copy = pltpu.make_async_copy(
                    kept.at[half, pl.ds(0, width)], part_outs[2 * place + j], sems.at[out_sem + 3 + 2 * place + j]
                )
                copy.start()
                finals.append(copy)
        for copy in finals:
            copy.wait()
    if not last:
        for i in range(3):
            pltpu.make_async_copy(acc_s.at[i], outs[0].at[i], sems.at[out_sem + i]).wait()


def expert_call(own, last, scal, blocks, wc, wd, acc, n_experts):
    tok = sum(b.shape[0] for b in blocks) // (2 * PLANE)
    units = tuple(b.shape[0] // (2 * tok) for b in blocks)
    both, width = wd.shape
    ff = both // 2
    cols = width // lax.axis_size("dp")
    rows = PLANE * tok
    anywhere = pl.BlockSpec(memory_space=pl.ANY)
    vmem = pl.BlockSpec(memory_space=pltpu.VMEM)
    args = [*blocks, wc, wd]
    if not own:
        args.append(acc)
    if last:
        out_shape = [jax.ShapeDtypeStruct((2, cols, ff), BF16)] * 2 + [jax.ShapeDtypeStruct((2, ff, cols), BF16)]
        out_specs = [vmem] * 3
    else:
        out_shape = [jax.ShapeDtypeStruct((3, cols, both), F32)]
        out_specs = [anywhere]
    if own:
        out_shape += [
            *[jax.ShapeDtypeStruct((rows // 2, width), BF16)] * 4,
            jax.ShapeDtypeStruct((n_experts, width), F32),
        ]
        out_specs += [anywhere] * 4 + [vmem]
    chunk = rows // 4
    scratch = [
        pltpu.VMEM((rows, width + LANES), BF16),
        pltpu.VMEM((rows, width), BF16),
        pltpu.VMEM((width, 2 * both + LANES), BF16),
        pltpu.VMEM((both, width), BF16),
        pltpu.VMEM((chunk, 2 * both + LANES), F32),
        pltpu.VMEM((rows, both), F32),
        pltpu.VMEM((2, rows, LANES), F32),
        pltpu.VMEM((3, cols, both), F32),
    ]
    if own:
        scratch += [pltpu.VMEM((rows, LANES), F32), pltpu.VMEM((2, rows, LANES), F32)]
    scratch += [pltpu.VMEM((rows, both), BF16), pltpu.VMEM((rows, 2 * both + 2 * LANES * own), BF16)]
    scratch.append(pltpu.SemaphoreType.DMA((2 * PLANE + 11,)))
    aliases = {} if own or last else {1 + len(blocks) + 2: 0}
    flops = 2 * rows * width * both * 3 + 2 * rows * cols * both * 3
    return pl.pallas_call(
        functools.partial(expert_kernel, own, last, tok, width, ff, cols, units),
        grid_spec=pltpu.PrefetchScalarGridSpec(
            num_scalar_prefetch=1,
            grid=(),
            in_specs=[anywhere] * len(args),
            out_specs=out_specs,
            scratch_shapes=scratch,
        ),
        out_shape=out_shape,
        input_output_aliases=aliases,
        compiler_params=pltpu.CompilerParams(vmem_limit_bytes=58 * 1024 * 1024),
        cost_estimate=pl.CostEstimate(flops=flops, bytes_accessed=40_000_000, transcendentals=rows * both),
        name="experts_own" if own else "experts_last" if last else "experts_mid",
    )(scal, *args)


def flip(x, even, odd):
    groups = lax.axis_size("expert")
    return lax.ppermute(x, "expert", [(i, i ^ (odd if i % 2 else even)) for i in range(groups)])


def dense_body(tokens, expert_ids, router, w_gate, w_up, w_down, out_grad):
    tok, width = tokens.shape
    n_experts = router.shape[1]
    ff = w_gate.shape[2]
    n_dp = lax.axis_size("dp")
    me = lax.axis_index("expert")
    core = me % 2
    ladder = jnp.arange(LANES, dtype=jnp.int32)
    mask = jnp.any(expert_ids[:, :, None] == ladder[None, None, :], axis=1).astype(BF16)
    block = jnp.concatenate(
        [
            jnp.concatenate([tokens, mask], axis=1),
            jnp.concatenate([out_grad, jnp.zeros((tok, LANES), BF16)], axis=1),
        ],
        axis=0,
    )
    router_pad = jnp.pad(router, ((0, 0), (0, LANES - n_experts)))
    wc = jnp.concatenate([w_gate[0], w_gate[1], w_up[0], w_up[1], router_pad, router_pad], axis=1)
    wd = w_down.reshape(2 * ff, width)
    near_at = jnp.where(core == 0, 1, 2)
    scal = jnp.stack(
        [me * 2, lax.axis_index("dp"), 0, 4, near_at, near_at + 4, 7 - near_at, 3 - near_at, 3, 7]
    ).astype(jnp.int32)
    ring = [(i, (i + 1) % n_dp) for i in range(n_dp)]

    def swap(b):
        return flip(b, 1, 1)

    def pair_of(b):
        return jnp.concatenate([b, swap(b)], axis=0)

    def over_link(b):
        return flip(b, 2, 4)

    def onward(near):
        return flip(near[: 2 * tok], 4, 2)

    def along(b):
        return lax.ppermute(b, "dp", ring)

    def hold(*values):
        return lax.optimization_barrier(values)

    def experts(g, acc, blocks):
        return expert_call(g == 0, g == n_dp - 1, scal, blocks, wc, wd, acc, n_experts)

    def rows_of(x, j):
        return x[j * tok : (j + 1) * tok].astype(F32)

    def core_sums(low, other):
        return [rows_of(low, 0) + rows_of(other, 0)] + [
            (rows_of(low, j) + rows_of(other, j)).astype(BF16) for j in range(1, 4)
        ]

    def plane_total(mine, arrived):
        for a in arrived:
            mine = mine + a.astype(F32)
        return mine.astype(BF16)

    one = along(block)
    pair0 = pair_of(block)
    near0 = over_link(pair0)
    near0, one, wc = hold(near0, one, wc)
    diag0, other0, two, pair1 = onward(near0), swap(near0), along(one), pair_of(one)
    diag0, other0, one, pair1 = hold(diag0, other0, one, pair1)
    blocks0 = [pair0, near0, other0, diag0, swap(diag0)]

    near1, diag1 = over_link(pair1), flip(one, 6, 6)
    acc, mixed_low, mixed_high, token_low, token_high, rp = experts(0, None, blocks0)
    acc, mixed_low, mixed_high, token_low, token_high, rp, near1, diag1, two = hold(
        acc, mixed_low, mixed_high, token_low, token_high, rp, near1, diag1, two
    )
    blocks1 = [pair1, near1, swap(near1), diag1, swap(diag1)]

    pair2 = pair_of(two)
    near2, three = over_link(pair2), along(two)
    rp = rp + swap(rp)
    mixed_other, token_other = swap(mixed_high), swap(token_high)
    (acc,) = experts(1, acc, blocks1)
    acc, near2, three, rp, mixed_other, token_other, mixed_low, token_low = hold(
        acc, near2, three, rp, mixed_other, token_other, mixed_low, token_low
    )

    diag2, other2, pair3 = onward(near2), swap(near2), pair_of(three)
    rp_z = lax.ppermute(rp, "dp", [(i, i ^ 1) for i in range(n_dp)])
    mixed_sums, token_sums = core_sums(mixed_low, mixed_other), core_sums(token_low, token_other)
    acc, diag2, other2, pair3, rp, rp_z, *sums = hold(
        acc, diag2, other2, pair3, rp, rp_z, *mixed_sums, *token_sums
    )
    mixed_sums, token_sums = sums[:4], sums[4:]
    blocks2 = [pair2, near2, other2, diag2, swap(diag2)]

    rp = rp + rp_z
    near3 = over_link(pair3)
    rp_z = lax.ppermute(rp, "dp", [(i, i ^ 2) for i in range(n_dp)])
    mixed_x, mixed_y = flip(mixed_sums[1], 2, 2), flip(mixed_sums[2], 4, 4)
    (acc,) = experts(2, acc, blocks2)
    acc, near3, mixed_x, mixed_y, rp, rp_z = hold(acc, near3, mixed_x, mixed_y, rp, rp_z)

    rp = rp + rp_z
    diag3, other3 = onward(near3), swap(near3)
    rp_x = flip(rp, 2, 2)
    acc, diag3, other3, rp, rp_x, mixed_d, token_3 = hold(
        acc, diag3, other3, rp, rp_x, mixed_sums[3], token_sums[3]
    )
    rp = rp + rp_x
    mixed_d = flip(mixed_d, 6, 6)
    token_parts = [flip(t, k, k) for t, k in zip((*token_sums[1:3], token_3), (2, 4, 6))]
    rp_y = flip(rp, 4, 4)
    out = experts(3, acc, [pair3, near3, other3, diag3, swap(diag3)])
    *out, mixed_d, rp_y, token_x, token_y, token_d = hold(*out, mixed_d, rp_y, *token_parts)
    mixed = plane_total(mixed_sums[0], (mixed_x, mixed_y, mixed_d))
    token_grad = plane_total(token_sums[0], (token_x, token_y, token_d))
    rp = rp + rp_y
    return (mixed, token_grad, rp.T, *out)


def flat_rows(array):
    return array.reshape(array.shape[0], array.shape[1] * array.shape[2], array.shape[3])


def sparse_body(tokens, expert_ids, router, w_gate, w_up, w_down, out_grad):
    f32 = jnp.float32
    bf16 = jnp.bfloat16
    tok_dev, width = tokens.shape
    top = expert_ids.shape[1]
    n_experts = router.shape[1]
    local_experts = w_gate.shape[0]
    groups = lax.axis_size("expert")
    capacity = (tok_dev * top * 9 + 8 * n_experts - 1) // (8 * n_experts)
    n_assign = tok_dev * top
    flat_ids = expert_ids.reshape(-1)
    ladder = jnp.arange(n_experts, dtype=jnp.int32)
    onehot = (flat_ids[:, None] == ladder[None, :]).astype(jnp.int32)
    rank = jnp.sum((jnp.cumsum(onehot, axis=0) - onehot) * onehot, axis=1)
    owner = flat_ids // local_experts
    within = flat_ids % local_experts
    dest = (within * groups + owner) * capacity + rank
    slot_src = jnp.full((n_experts * capacity,), n_assign, jnp.int32)
    slot_src = slot_src.at[dest].set(jnp.arange(n_assign, dtype=jnp.int32))
    live = slot_src < n_assign
    slot_tok = jnp.where(live, slot_src // top, 0)
    logits = jnp.dot(tokens, router, preferred_element_type=f32)
    scores = jax.nn.sigmoid(logits)
    chosen = jnp.take_along_axis(scores, expert_ids, axis=1)
    total = jnp.sum(chosen, axis=1, keepdims=True)
    gates = chosen / total
    gate_slots = jnp.where(live, gates.reshape(-1)[jnp.minimum(slot_src, n_assign - 1)], 0.0)
    send = jnp.where(live[:, None], tokens[slot_tok], jnp.zeros((), bf16))
    send = send.reshape(local_experts, groups, capacity, width)
    piece = lax.all_to_all(send, "expert", split_axis=1, concat_axis=1, tiled=True)
    shape = piece.shape
    rows = flat_rows(piece)
    pre_gate = jnp.einsum("jrd,jdf->jrf", rows, w_gate, preferred_element_type=f32)
    pre_up = jnp.einsum("jrd,jdf->jrf", rows, w_up, preferred_element_type=f32)
    hidden = (pre_gate * jax.nn.sigmoid(pre_gate) * pre_up).astype(bf16)
    expert_out = jnp.einsum("jrf,jfd->jrd", hidden, w_down, preferred_element_type=f32).astype(bf16)
    hid_shape = (shape[0], shape[1], shape[2], hidden.shape[2])
    expert_out = expert_out.reshape(shape)
    hidden = hidden.reshape(hid_shape)
    results = (expert_out, hidden, piece, pre_gate.reshape(hid_shape), pre_up.reshape(hid_shape))
    expert_out = results[0]
    hidden = flat_rows(results[1])
    back = lax.all_to_all(expert_out, "expert", split_axis=1, concat_axis=1, tiled=True).reshape(
        n_experts * capacity, width
    )
    picked = back[dest].reshape(tok_dev, top, width)
    mixed = jnp.einsum("tk,tkd->td", gates, picked.astype(f32)).astype(bf16)
    gate_sens = jnp.einsum("tkd,td->tk", picked, out_grad, preferred_element_type=f32)
    grad_rows = (gate_slots[:, None] * out_grad[slot_tok].astype(f32)).astype(bf16)
    grad_send = jnp.where(live[:, None], grad_rows, jnp.zeros((), bf16))
    grad_send = grad_send.reshape(local_experts, groups, capacity, width)
    grad_in4 = lax.all_to_all(grad_send, "expert", split_axis=1, concat_axis=1, tiled=True)
    grad_in = flat_rows(grad_in4)
    pre_gate = flat_rows(results[3])
    pre_up = flat_rows(results[4])
    hidden_grad = jnp.einsum("jrd,jfd->jrf", grad_in, w_down, preferred_element_type=f32)
    sig = jax.nn.sigmoid(pre_gate)
    silu_val = pre_gate * sig
    gate_term = (hidden_grad * pre_up * sig * (1.0 + pre_gate * (1.0 - sig))).astype(bf16)
    up_term = (hidden_grad * silu_val).astype(bf16)
    input_grad = (
        jnp.einsum("jrf,jdf->jrd", gate_term, w_gate, preferred_element_type=f32)
        + jnp.einsum("jrf,jdf->jrd", up_term, w_up, preferred_element_type=f32)
    ).astype(bf16)
    input_grad = input_grad.reshape(grad_in4.shape)
    returned = lax.all_to_all(
        input_grad, "expert", split_axis=1, concat_axis=1, tiled=True
    ).reshape(n_experts * capacity, width)
    moe_grad = jnp.sum(returned[dest].reshape(tok_dev, top, width).astype(f32), axis=1)
    chosen_grad = (gate_sens - jnp.sum(gate_sens * gates, axis=1, keepdims=True)) / total
    sel_grad = chosen_grad * chosen * (1.0 - chosen)
    pick = (expert_ids[:, :, None] == ladder[None, None, :]).astype(f32)
    logit_grad = jnp.einsum("tk,tke->te", sel_grad, pick).astype(bf16)
    token_grad = (moe_grad + jnp.dot(logit_grad, router.T, preferred_element_type=f32)).astype(bf16)
    router_grad = lax.psum(
        jnp.dot(tokens.T, logit_grad, preferred_element_type=f32), ("expert", "dp")
    )
    hidden_width = hidden.shape[2]
    arrived4 = results[2]
    columns = (
        lax.all_to_all(arrived4, "dp", split_axis=3, concat_axis=1, tiled=True),
        lax.all_to_all(grad_in4, "dp", split_axis=3, concat_axis=1, tiled=True),
    )
    hid_shape = (local_experts, groups, capacity, hidden_width)
    hiddens = (
        lax.all_gather(gate_term.reshape(hid_shape), "dp", axis=1, tiled=True),
        lax.all_gather(up_term.reshape(hid_shape), "dp", axis=1, tiled=True),
        lax.all_gather(results[1], "dp", axis=1, tiled=True),
    )
    x_cols = flat_rows(columns[0])
    g_cols = flat_rows(columns[1])
    gate_grad = jnp.einsum(
        "jrd,jrf->jdf", x_cols, flat_rows(hiddens[0]), preferred_element_type=f32
    ).astype(bf16)
    up_grad = jnp.einsum(
        "jrd,jrf->jdf", x_cols, flat_rows(hiddens[1]), preferred_element_type=f32
    ).astype(bf16)
    down_grad = jnp.einsum(
        "jrf,jrd->jfd", flat_rows(hiddens[2]), g_cols, preferred_element_type=f32
    ).astype(bf16)
    return (mixed, token_grad, router_grad, gate_grad, up_grad, down_grad)


def body(*args):
    plane = lax.axis_size("expert") == 8 and args[3].shape[0] == 2
    line = lax.axis_size("dp")
    return (dense_body if plane and line == 4 else sparse_body)(*args)


def solution(mesh):
    placed = (
        P(("expert", "dp"), None),
        P(("expert", "dp"), None),
        P(),
        P("expert", None, None),
        P("expert", None, None),
        P("expert", None, None),
        P(("expert", "dp"), None),
    )
    return jax.shard_map(
        body,
        mesh=mesh,
        in_specs=placed,
        out_specs=(
            P(("expert", "dp"), None),
            P(("expert", "dp"), None),
            P(),
            P("expert", "dp", None),
            P("expert", "dp", None),
            P("expert", None, "dp"),
        ),
        check_vma=False,
    )
```

```python
import functools

import jax
import jax.numpy as jnp
from jax import lax
from jax.experimental import pallas as pl
from jax.experimental.pallas import tpu as pltpu
from jax.sharding import PartitionSpec as P

F32 = jnp.float32
BF16 = jnp.bfloat16
LANES = 128
PLANE = 8


def mm(a, b, contract):
    return lax.dot_general(a, b, (contract, ((), ())), preferred_element_type=F32)


NN = ((1,), (0,))
NT = ((1,), (1,))
TN = ((0,), (0,))


def expert_kernel(own, last, tok, width, ff, cols, units, *refs):
    refs = list(refs)
    scal = refs.pop(0)
    blocks = [refs.pop(0) for _ in units]
    wc, wd = refs.pop(0), refs.pop(0)
    acc_in = None if own else refs.pop(0)
    outs = [refs.pop(0) for _ in range(3 if last else 1)]
    if own:
        part_outs, rp_out = [refs.pop(0) for _ in range(4)], refs.pop(0)
    x_s, o_s, wc_s, wd_s, pre_s, q_s, gb, acc_s = (refs.pop(0) for _ in range(8))
    if own:
        a_s, sacc = refs.pop(0), refs.pop(0)
    hid, gu = refs.pop(0), refs.pop(0)
    sems = refs.pop(0)
    rows = PLANE * tok
    both = 2 * ff
    chunk_rows = pre_s.shape[0]
    first_expert = scal[0]
    zcol = pl.multiple_of(scal[1] * cols, LANES)
    tiles_e = ff // LANES

    taken = iter(range(64))
    x_copies, o_copies = [], []
    place = 2
    for ref, count in zip(blocks, units):
        for u in range(count):
            at = pl.ds(pl.multiple_of(scal[place] * tok, tok), tok)
            place += 1
            base = 2 * tok * u
            x_copies.append(
                pltpu.make_async_copy(ref.at[pl.ds(base, tok), :], x_s.at[at, :], sems.at[next(taken)])
            )
            o_copies.append(
                pltpu.make_async_copy(
                    ref.at[pl.ds(base + tok, tok), pl.ds(0, width)], o_s.at[at, :], sems.at[next(taken)]
                )
            )

    def part(src, dst, lo, size):
        return pltpu.make_async_copy(
            src.at[:, pl.ds(lo, size)], dst.at[:, pl.ds(lo, size)], sems.at[next(taken)]
        )

    gate_copy = part(wc, wc_s, 0, both)
    up_copy = part(wc, wc_s, both, both + LANES)
    wd_copy = pltpu.make_async_copy(wd, wd_s, sems.at[next(taken)])
    acc_copies = []
    if not own:
        acc_copies = [pltpu.make_async_copy(acc_in, acc_s, sems.at[next(taken)])]
    for copy in [*o_copies, wd_copy, *x_copies, gate_copy, up_copy, *acc_copies]:
        copy.start()
    out_sem = next(taken)
    for copy in [*o_copies, wd_copy]:
        copy.wait()

    def back(c, carry):
        here = pl.ds(pl.multiple_of(c * chunk_rows, chunk_rows), chunk_rows)
        q_s[here, :] = mm(o_s[here, :], wd_s[...], NT)
        return carry

    lax.fori_loop(0, rows // chunk_rows, back, 0)
    for copy in [*x_copies, gate_copy, up_copy]:
        copy.wait()

    lane = lax.broadcasted_iota(jnp.int32, (chunk_rows, LANES), 1)

    def chunk(c, carry):
        here = pl.ds(pl.multiple_of(c * chunk_rows, chunk_rows), chunk_rows)
        pre_s[...] = mm(x_s[here, :width], wc_s[...], NN)
        score = jax.nn.sigmoid(pre_s[:, 2 * both :])
        chosen = score * x_s[here, width:].astype(F32)
        gates = chosen / jnp.sum(chosen, axis=1, keepdims=True)
        for j in range(2):
            col = jnp.sum(jnp.where(lane == first_expert + j, gates, 0.0), axis=1, keepdims=True)
            gb[j, here, :] = jnp.broadcast_to(col, (chunk_rows, LANES))
        if own:
            a_s[here, :] = gates * (1.0 - score)
            sacc[:, here, :] = jnp.zeros((2, chunk_rows, LANES), F32)

        def piece(i, carry):
            r = pl.ds(pl.multiple_of(i * LANES, LANES), LANES)
            ra = pl.ds(pl.multiple_of(c * chunk_rows + i * LANES, LANES), LANES)
            for t in range(both // LANES):
                expert = t // tiles_e
                gate = gb[expert, ra, :]
                pre = pre_s[r, t * LANES : (t + 1) * LANES]
                up = pre_s[r, both + t * LANES : both + (t + 1) * LANES]
                q = q_s[ra, t * LANES : (t + 1) * LANES]
                sig = 0.5 * jnp.tanh(0.5 * pre) + 0.5
                silu = pre * sig
                h = silu * up
                gq = gate * q
                hid[ra, t * LANES : (t + 1) * LANES] = (gate * h).astype(BF16)
                gu[ra, t * LANES : (t + 1) * LANES] = (gq * up * (sig + silu * (1.0 - sig))).astype(BF16)
                gu[ra, both + t * LANES : both + (t + 1) * LANES] = (gq * silu).astype(BF16)
                if own:
                    sacc[expert, ra, :] += h * q
            return carry

        lax.fori_loop(0, chunk_rows // LANES, piece, 0)
        return carry

    lax.fori_loop(0, rows // chunk_rows, chunk, 0)

    for copy in acc_copies:
        copy.wait()
    def weight_grad(i, grad):
        if not own:
            grad = grad + acc_s[i]
        acc_s[i] = grad
        if not last:
            pltpu.make_async_copy(acc_s.at[i], outs[0].at[i], sems.at[out_sem + i]).start()

    def from_tokens(i, carry):
        part = pl.ds(pl.multiple_of(i * both, LANES), both)
        weight_grad(i, mm(x_s[:, pl.ds(zcol, cols)], gu[:, part], TN))
        return carry

    lax.fori_loop(0, 2, from_tokens, 0)
    weight_grad(2, mm(o_s[:, pl.ds(zcol, cols)], hid[...], TN))
    if last:
        for i in range(2):
            for e in range(2):
                outs[i][e] = acc_s[i, :, e * ff : (e + 1) * ff].astype(BF16)
        for e in range(2):
            outs[2][e] = acc_s[2, :, e * ff : (e + 1) * ff].T.astype(BF16)

    if own:
        lane = lax.broadcasted_iota(jnp.int32, (rows, LANES), 1)
        term = jnp.zeros((rows, LANES), F32)
        shared = jnp.zeros((rows, LANES), F32)
        for j in range(2):
            sens = jnp.sum(sacc[j], axis=1, keepdims=True)
            term = term + jnp.where(lane == first_expert + j, sens, 0.0)
            shared = shared + gb[j] * sens
        grad = a_s[...] * (term - shared)
        high = grad.astype(BF16)
        low = (grad - high.astype(F32)).astype(BF16)
        gu[:, 2 * both : 2 * both + LANES] = high
        gu[:, 2 * both + LANES :] = low
        n_out = rp_out.shape[0]
        split = gu[:, 2 * both :]
        terms = mm(split, x_s[:, :width], TN)
        rp_out[...] = terms[:n_out] + terms[LANES : LANES + n_out]

        def mix(c, carry):
            here = pl.ds(pl.multiple_of(c * chunk_rows, chunk_rows), chunk_rows)
            o_s[here, :] = mm(hid[here, :], wd_s[...], NN).astype(BF16)
            return carry

        def token(c, carry):
            here = pl.ds(pl.multiple_of(c * chunk_rows, chunk_rows), chunk_rows)
            grad = mm(gu[here, : 2 * both + LANES], wc_s[...], NT)
            x_s[here, :width] = (grad + mm(gu[here, 2 * both + LANES :], wc_s[:, 2 * both :], NT)).astype(BF16)
            return carry

        finals = []
        for place, (step, kept) in enumerate(((mix, o_s), (token, x_s))):
            lax.fori_loop(0, rows // chunk_rows, step, 0)
            for j in range(2):
                half = pl.ds(j * rows // 2, rows // 2)
                copy = pltpu.make_async_copy(
                    kept.at[half, pl.ds(0, width)], part_outs[2 * place + j], sems.at[out_sem + 3 + 2 * place + j]
                )
                copy.start()
                finals.append(copy)
        for copy in finals:
            copy.wait()
    if not last:
        for i in range(3):
            pltpu.make_async_copy(acc_s.at[i], outs[0].at[i], sems.at[out_sem + i]).wait()


def expert_call(own, last, scal, blocks, wc, wd, acc, n_experts):
    tok = sum(b.shape[0] for b in blocks) // (2 * PLANE)
    units = tuple(b.shape[0] // (2 * tok) for b in blocks)
    both, width = wd.shape
    ff = both // 2
    cols = width // lax.axis_size("dp")
    rows = PLANE * tok
    anywhere = pl.BlockSpec(memory_space=pl.ANY)
    vmem = pl.BlockSpec(memory_space=pltpu.VMEM)
    args = [*blocks, wc, wd]
    if not own:
        args.append(acc)
    if last:
        out_shape = [jax.ShapeDtypeStruct((2, cols, ff), BF16)] * 2 + [jax.ShapeDtypeStruct((2, ff, cols), BF16)]
        out_specs = [vmem] * 3
    else:
        out_shape = [jax.ShapeDtypeStruct((3, cols, both), F32)]
        out_specs = [anywhere]
    if own:
        out_shape += [
            *[jax.ShapeDtypeStruct((rows // 2, width), BF16)] * 4,
            jax.ShapeDtypeStruct((n_experts, width), F32),
        ]
        out_specs += [anywhere] * 4 + [vmem]
    chunk = rows // 4
    scratch = [
        pltpu.VMEM((rows, width + LANES), BF16),
        pltpu.VMEM((rows, width), BF16),
        pltpu.VMEM((width, 2 * both + LANES), BF16),
        pltpu.VMEM((both, width), BF16),
        pltpu.VMEM((chunk, 2 * both + LANES), F32),
        pltpu.VMEM((rows, both), F32),
        pltpu.VMEM((2, rows, LANES), F32),
        pltpu.VMEM((3, cols, both), F32),
    ]
    if own:
        scratch += [pltpu.VMEM((rows, LANES), F32), pltpu.VMEM((2, rows, LANES), F32)]
    scratch += [pltpu.VMEM((rows, both), BF16), pltpu.VMEM((rows, 2 * both + 2 * LANES * own), BF16)]
    scratch.append(pltpu.SemaphoreType.DMA((2 * PLANE + 11,)))
    aliases = {} if own or last else {1 + len(blocks) + 2: 0}
    flops = 2 * rows * width * both * 3 + 2 * rows * cols * both * 3
    return pl.pallas_call(
        functools.partial(expert_kernel, own, last, tok, width, ff, cols, units),
        grid_spec=pltpu.PrefetchScalarGridSpec(
            num_scalar_prefetch=1,
            grid=(),
            in_specs=[anywhere] * len(args),
            out_specs=out_specs,
            scratch_shapes=scratch,
        ),
        out_shape=out_shape,
        input_output_aliases=aliases,
        compiler_params=pltpu.CompilerParams(vmem_limit_bytes=58 * 1024 * 1024),
        cost_estimate=pl.CostEstimate(flops=flops, bytes_accessed=40_000_000, transcendentals=rows * both),
        name="experts_own" if own else "experts_last" if last else "experts_mid",
    )(scal, *args)


def flip(x, even, odd):
    groups = lax.axis_size("expert")
    return lax.ppermute(x, "expert", [(i, i ^ (odd if i % 2 else even)) for i in range(groups)])


def dense_body(tokens, expert_ids, router, w_gate, w_up, w_down, out_grad):
    tok, width = tokens.shape
    n_experts = router.shape[1]
    ff = w_gate.shape[2]
    n_dp = lax.axis_size("dp")
    me = lax.axis_index("expert")
    core = me % 2
    ladder = jnp.arange(LANES, dtype=jnp.int32)
    mask = jnp.any(expert_ids[:, :, None] == ladder[None, None, :], axis=1).astype(BF16)
    block = jnp.concatenate(
        [
            jnp.concatenate([tokens, mask], axis=1),
            jnp.concatenate([out_grad, jnp.zeros((tok, LANES), BF16)], axis=1),
        ],
        axis=0,
    )
    router_pad = jnp.pad(router, ((0, 0), (0, LANES - n_experts)))
    wc = jnp.concatenate([w_gate[0], w_gate[1], w_up[0], w_up[1], router_pad, router_pad], axis=1)
    wd = w_down.reshape(2 * ff, width)
    near_at = jnp.where(core == 0, 1, 2)
    scal = jnp.stack(
        [me * 2, lax.axis_index("dp"), 0, 4, near_at, near_at + 4, 7 - near_at, 3 - near_at, 3, 7]
    ).astype(jnp.int32)
    ring = [(i, (i + 1) % n_dp) for i in range(n_dp)]

    def swap(b):
        return flip(b, 1, 1)

    def pair_of(b):
        return jnp.concatenate([b, swap(b)], axis=0)

    def over_link(b):
        return flip(b, 2, 4)

    def onward(near):
        return flip(near[: 2 * tok], 4, 2)

    def along(b):
        return lax.ppermute(b, "dp", ring)

    def hold(*values):
        return lax.optimization_barrier(values)

    def experts(g, acc, blocks):
        return expert_call(g == 0, g == n_dp - 1, scal, blocks, wc, wd, acc, n_experts)

    def rows_of(x, j):
        return x[j * tok : (j + 1) * tok].astype(F32)

    def core_sums(low, other):
        return [rows_of(low, 0) + rows_of(other, 0)] + [
            (rows_of(low, j) + rows_of(other, j)).astype(BF16) for j in range(1, 4)
        ]

    def plane_total(mine, arrived):
        for a in arrived:
            mine = mine + a.astype(F32)
        return mine.astype(BF16)

    one = along(block)
    pair0 = pair_of(block)
    near0 = over_link(pair0)
    near0, one, wc = hold(near0, one, wc)
    diag0, other0, two, pair1 = onward(near0), swap(near0), along(one), pair_of(one)
    diag0, other0, one, pair1, two = hold(diag0, other0, one, pair1, two)
    blocks0 = [pair0, near0, other0, diag0, swap(diag0)]

    near1, diag1 = over_link(pair1), along(diag0)
    three, sibling2 = along(two), swap(two)
    acc, mixed_low, mixed_high, token_low, token_high, rp = experts(0, None, blocks0)
    acc, mixed_low, mixed_high, token_low, token_high, rp, near1, diag1, three, sibling2 = hold(
        acc, mixed_low, mixed_high, token_low, token_high, rp, near1, diag1, three, sibling2
    )
    blocks1 = [pair1, near1, swap(near1), diag1, swap(diag1)]

    pair2 = jnp.concatenate([two, sibling2], axis=0)
    near2, diag2 = over_link(pair2), along(diag1)
    pair3 = pair_of(three)
    rp = rp + swap(rp)
    rp_z = lax.ppermute(rp, "dp", [(i, i ^ 1) for i in range(n_dp)])
    mixed_other, token_other = swap(mixed_high), swap(token_high)
    (acc,) = experts(1, acc, blocks1)
    acc, near2, diag2, pair3, rp, rp_z, mixed_other, token_other, mixed_low, token_low = hold(
        acc, near2, diag2, pair3, rp, rp_z, mixed_other, token_other, mixed_low, token_low
    )
    blocks2 = [pair2, near2, swap(near2), diag2, swap(diag2)]

    rp = rp + rp_z
    rp_z = lax.ppermute(rp, "dp", [(i, i ^ 2) for i in range(n_dp)])
    near3, diag3 = over_link(pair3), along(diag2)
    mixed_sums = core_sums(mixed_low, mixed_other)
    mixed_x, mixed_y = flip(mixed_sums[1], 2, 2), flip(mixed_sums[2], 4, 4)
    (acc,) = experts(2, acc, blocks2)
    acc, near3, diag3, mixed_x, mixed_y, rp, rp_z, mixed_d, token_low, token_other = hold(
        acc, near3, diag3, mixed_x, mixed_y, rp, rp_z, mixed_sums[3], token_low, token_other
    )

    rp = rp + rp_z
    rp_x = flip(rp, 2, 2)
    token_sums = core_sums(token_low, token_other)
    mixed_d = flip(mixed_d, 6, 6)
    token_parts = [flip(t, k, k) for t, k in zip(token_sums[1:], (2, 4, 6))]
    out = experts(3, acc, [pair3, near3, swap(near3), diag3, swap(diag3)])
    *out, rp, rp_x, mixed_d, token_x, token_y, token_d = hold(*out, rp, rp_x, mixed_d, *token_parts)
    rp = rp + rp_x
    rp_y = flip(rp, 4, 4)
    mixed = plane_total(mixed_sums[0], (mixed_x, mixed_y, mixed_d))
    token_grad = plane_total(token_sums[0], (token_x, token_y, token_d))
    rp = rp + rp_y
    return (mixed, token_grad, rp.T, *out)


def flat_rows(array):
    return array.reshape(array.shape[0], array.shape[1] * array.shape[2], array.shape[3])


def sparse_body(tokens, expert_ids, router, w_gate, w_up, w_down, out_grad):
    f32 = jnp.float32
    bf16 = jnp.bfloat16
    tok_dev, width = tokens.shape
    top = expert_ids.shape[1]
    n_experts = router.shape[1]
    local_experts = w_gate.shape[0]
    groups = lax.axis_size("expert")
    capacity = (tok_dev * top * 9 + 8 * n_experts - 1) // (8 * n_experts)
    n_assign = tok_dev * top
    flat_ids = expert_ids.reshape(-1)
    ladder = jnp.arange(n_experts, dtype=jnp.int32)
    onehot = (flat_ids[:, None] == ladder[None, :]).astype(jnp.int32)
    rank = jnp.sum((jnp.cumsum(onehot, axis=0) - onehot) * onehot, axis=1)
    owner = flat_ids // local_experts
    within = flat_ids % local_experts
    dest = (within * groups + owner) * capacity + rank
    slot_src = jnp.full((n_experts * capacity,), n_assign, jnp.int32)
    slot_src = slot_src.at[dest].set(jnp.arange(n_assign, dtype=jnp.int32))
    live = slot_src < n_assign
    slot_tok = jnp.where(live, slot_src // top, 0)
    logits = jnp.dot(tokens, router, preferred_element_type=f32)
    scores = jax.nn.sigmoid(logits)
    chosen = jnp.take_along_axis(scores, expert_ids, axis=1)
    total = jnp.sum(chosen, axis=1, keepdims=True)
    gates = chosen / total
    gate_slots = jnp.where(live, gates.reshape(-1)[jnp.minimum(slot_src, n_assign - 1)], 0.0)
    send = jnp.where(live[:, None], tokens[slot_tok], jnp.zeros((), bf16))
    send = send.reshape(local_experts, groups, capacity, width)
    piece = lax.all_to_all(send, "expert", split_axis=1, concat_axis=1, tiled=True)
    shape = piece.shape
    rows = flat_rows(piece)
    pre_gate = jnp.einsum("jrd,jdf->jrf", rows, w_gate, preferred_element_type=f32)
    pre_up = jnp.einsum("jrd,jdf->jrf", rows, w_up, preferred_element_type=f32)
    hidden = (pre_gate * jax.nn.sigmoid(pre_gate) * pre_up).astype(bf16)
    expert_out = jnp.einsum("jrf,jfd->jrd", hidden, w_down, preferred_element_type=f32).astype(bf16)
    hid_shape = (shape[0], shape[1], shape[2], hidden.shape[2])
    expert_out = expert_out.reshape(shape)
    hidden = hidden.reshape(hid_shape)
    results = (expert_out, hidden, piece, pre_gate.reshape(hid_shape), pre_up.reshape(hid_shape))
    expert_out = results[0]
    hidden = flat_rows(results[1])
    back = lax.all_to_all(expert_out, "expert", split_axis=1, concat_axis=1, tiled=True).reshape(
        n_experts * capacity, width
    )
    picked = back[dest].reshape(tok_dev, top, width)
    mixed = jnp.einsum("tk,tkd->td", gates, picked.astype(f32)).astype(bf16)
    gate_sens = jnp.einsum("tkd,td->tk", picked, out_grad, preferred_element_type=f32)
    grad_rows = (gate_slots[:, None] * out_grad[slot_tok].astype(f32)).astype(bf16)
    grad_send = jnp.where(live[:, None], grad_rows, jnp.zeros((), bf16))
    grad_send = grad_send.reshape(local_experts, groups, capacity, width)
    grad_in4 = lax.all_to_all(grad_send, "expert", split_axis=1, concat_axis=1, tiled=True)
    grad_in = flat_rows(grad_in4)
    pre_gate = flat_rows(results[3])
    pre_up = flat_rows(results[4])
    hidden_grad = jnp.einsum("jrd,jfd->jrf", grad_in, w_down, preferred_element_type=f32)
    sig = jax.nn.sigmoid(pre_gate)
    silu_val = pre_gate * sig
    gate_term = (hidden_grad * pre_up * sig * (1.0 + pre_gate * (1.0 - sig))).astype(bf16)
    up_term = (hidden_grad * silu_val).astype(bf16)
    input_grad = (
        jnp.einsum("jrf,jdf->jrd", gate_term, w_gate, preferred_element_type=f32)
        + jnp.einsum("jrf,jdf->jrd", up_term, w_up, preferred_element_type=f32)
    ).astype(bf16)
    input_grad = input_grad.reshape(grad_in4.shape)
    returned = lax.all_to_all(
        input_grad, "expert", split_axis=1, concat_axis=1, tiled=True
    ).reshape(n_experts * capacity, width)
    moe_grad = jnp.sum(returned[dest].reshape(tok_dev, top, width).astype(f32), axis=1)
    chosen_grad = (gate_sens - jnp.sum(gate_sens * gates, axis=1, keepdims=True)) / total
    sel_grad = chosen_grad * chosen * (1.0 - chosen)
    pick = (expert_ids[:, :, None] == ladder[None, None, :]).astype(f32)
    logit_grad = jnp.einsum("tk,tke->te", sel_grad, pick).astype(bf16)
    token_grad = (moe_grad + jnp.dot(logit_grad, router.T, preferred_element_type=f32)).astype(bf16)
    router_grad = lax.psum(
        jnp.dot(tokens.T, logit_grad, preferred_element_type=f32), ("expert", "dp")
    )
    hidden_width = hidden.shape[2]
    arrived4 = results[2]
    columns = (
        lax.all_to_all(arrived4, "dp", split_axis=3, concat_axis=1, tiled=True),
        lax.all_to_all(grad_in4, "dp", split_axis=3, concat_axis=1, tiled=True),
    )
    hid_shape = (local_experts, groups, capacity, hidden_width)
    hiddens = (
        lax.all_gather(gate_term.reshape(hid_shape), "dp", axis=1, tiled=True),
        lax.all_gather(up_term.reshape(hid_shape), "dp", axis=1, tiled=True),
        lax.all_gather(results[1], "dp", axis=1, tiled=True),
    )
    x_cols = flat_rows(columns[0])
    g_cols = flat_rows(columns[1])
    gate_grad = jnp.einsum(
        "jrd,jrf->jdf", x_cols, flat_rows(hiddens[0]), preferred_element_type=f32
    ).astype(bf16)
    up_grad = jnp.einsum(
        "jrd,jrf->jdf", x_cols, flat_rows(hiddens[1]), preferred_element_type=f32
    ).astype(bf16)
    down_grad = jnp.einsum(
        "jrf,jrd->jfd", flat_rows(hiddens[2]), g_cols, preferred_element_type=f32
    ).astype(bf16)
    return (mixed, token_grad, router_grad, gate_grad, up_grad, down_grad)


def body(*args):
    plane = lax.axis_size("expert") == 8 and args[3].shape[0] == 2
    line = lax.axis_size("dp")
    return (dense_body if plane and line == 4 else sparse_body)(*args)


def solution(mesh):
    placed = (
        P(("expert", "dp"), None),
        P(("expert", "dp"), None),
        P(),
        P("expert", None, None),
        P("expert", None, None),
        P("expert", None, None),
        P(("expert", "dp"), None),
    )
    return jax.shard_map(
        body,
        mesh=mesh,
        in_specs=placed,
        out_specs=(
            P(("expert", "dp"), None),
            P(("expert", "dp"), None),
            P(),
            P("expert", "dp", None),
            P("expert", "dp", None),
            P("expert", None, "dp"),
        ),
        check_vma=False,
    )
```

```python
import functools

import jax
import jax.numpy as jnp
from jax import lax
from jax.experimental import pallas as pl
from jax.experimental.pallas import tpu as pltpu
from jax.sharding import PartitionSpec as P

F32 = jnp.float32
BF16 = jnp.bfloat16
LANES = 128
PLANE = 8


def mm(a, b, contract):
    return lax.dot_general(a, b, (contract, ((), ())), preferred_element_type=F32)


NN = ((1,), (0,))
NT = ((1,), (1,))
TN = ((0,), (0,))


def expert_kernel(own, last, tok, width, ff, cols, units, *refs):
    refs = list(refs)
    scal = refs.pop(0)
    blocks = [refs.pop(0) for _ in units]
    wc, wd = refs.pop(0), refs.pop(0)
    acc_in = None if own else refs.pop(0)
    outs = [refs.pop(0) for _ in range(3 if last else 1)]
    if own:
        part_outs, rp_out = [refs.pop(0) for _ in range(4)], refs.pop(0)
    x_s, o_s, wc_s, wd_s, pre_s, q_s, gb, acc_s = (refs.pop(0) for _ in range(8))
    if own:
        a_s, sacc = refs.pop(0), refs.pop(0)
    hid, gu = refs.pop(0), refs.pop(0)
    sems = refs.pop(0)
    rows = PLANE * tok
    both = 2 * ff
    chunk_rows = pre_s.shape[0]
    first_expert = scal[0]
    zcol = pl.multiple_of(scal[1] * cols, LANES)
    tiles_e = ff // LANES

    taken = iter(range(64))
    x_copies, o_copies = [], []
    place = 2
    for ref, count in zip(blocks, units):
        for u in range(count):
            at = pl.ds(pl.multiple_of(scal[place] * tok, tok), tok)
            place += 1
            base = 2 * tok * u
            x_copies.append(
                pltpu.make_async_copy(ref.at[pl.ds(base, tok), :], x_s.at[at, :], sems.at[next(taken)])
            )
            o_copies.append(
                pltpu.make_async_copy(
                    ref.at[pl.ds(base + tok, tok), pl.ds(0, width)], o_s.at[at, :], sems.at[next(taken)]
                )
            )

    def part(src, dst, lo, size):
        return pltpu.make_async_copy(
            src.at[:, pl.ds(lo, size)], dst.at[:, pl.ds(lo, size)], sems.at[next(taken)]
        )

    gate_copy = part(wc, wc_s, 0, both)
    up_copy = part(wc, wc_s, both, both + LANES + LANES * own)
    wd_copy = pltpu.make_async_copy(wd, wd_s, sems.at[next(taken)])
    acc_copies = []
    if not own:
        acc_copies = [pltpu.make_async_copy(acc_in, acc_s, sems.at[next(taken)])]
    for copy in [*o_copies, wd_copy, *x_copies, gate_copy, up_copy, *acc_copies]:
        copy.start()
    out_sem = next(taken)
    for copy in [*o_copies, wd_copy]:
        copy.wait()

    def back(c, carry):
        here = pl.ds(pl.multiple_of(c * chunk_rows, chunk_rows), chunk_rows)
        q_s[here, :] = mm(o_s[here, :], wd_s[...], NT)
        return carry

    lax.fori_loop(0, rows // chunk_rows, back, 0)
    for copy in [*x_copies, gate_copy, up_copy]:
        copy.wait()

    lane = lax.broadcasted_iota(jnp.int32, (chunk_rows, LANES), 1)

    def chunk(c, carry):
        here = pl.ds(pl.multiple_of(c * chunk_rows, chunk_rows), chunk_rows)
        pre_s[...] = mm(x_s[here, :width], wc_s[:, : 2 * both + LANES], NN)
        score = jax.nn.sigmoid(pre_s[:, 2 * both :])
        chosen = score * x_s[here, width:].astype(F32)
        gates = chosen / jnp.sum(chosen, axis=1, keepdims=True)
        for j in range(2):
            col = jnp.sum(jnp.where(lane == first_expert + j, gates, 0.0), axis=1, keepdims=True)
            gb[j, here, :] = jnp.broadcast_to(col, (chunk_rows, LANES))
        if own:
            a_s[here, :] = gates * (1.0 - score)
            sacc[:, here, :] = jnp.zeros((2, chunk_rows, LANES), F32)

        def piece(i, carry):
            r = pl.ds(pl.multiple_of(i * LANES, LANES), LANES)
            ra = pl.ds(pl.multiple_of(c * chunk_rows + i * LANES, LANES), LANES)
            for t in range(both // LANES):
                expert = t // tiles_e
                gate = gb[expert, ra, :]
                pre = pre_s[r, t * LANES : (t + 1) * LANES]
                up = pre_s[r, both + t * LANES : both + (t + 1) * LANES]
                q = q_s[ra, t * LANES : (t + 1) * LANES]
                sig = 0.5 * jnp.tanh(0.5 * pre) + 0.5
                silu = pre * sig
                h = silu * up
                gq = gate * q
                hid[ra, t * LANES : (t + 1) * LANES] = (gate * h).astype(BF16)
                gu[ra, t * LANES : (t + 1) * LANES] = (gq * up * (sig + silu * (1.0 - sig))).astype(BF16)
                gu[ra, both + t * LANES : both + (t + 1) * LANES] = (gq * silu).astype(BF16)
                if own:
                    sacc[expert, ra, :] += h * q
            return carry

        lax.fori_loop(0, chunk_rows // LANES, piece, 0)
        return carry

    lax.fori_loop(0, rows // chunk_rows, chunk, 0)

    for copy in acc_copies:
        copy.wait()
    def weight_grad(i, grad):
        if not own:
            grad = grad + acc_s[i]
        acc_s[i] = grad
        if not last:
            pltpu.make_async_copy(acc_s.at[i], outs[0].at[i], sems.at[out_sem + i]).start()

    def from_tokens(i, carry):
        part = pl.ds(pl.multiple_of(i * both, LANES), both)
        weight_grad(i, mm(x_s[:, pl.ds(zcol, cols)], gu[:, part], TN))
        return carry

    lax.fori_loop(0, 2, from_tokens, 0)
    weight_grad(2, mm(o_s[:, pl.ds(zcol, cols)], hid[...], TN))
    if last:
        for i in range(2):
            for e in range(2):
                outs[i][e] = acc_s[i, :, e * ff : (e + 1) * ff].astype(BF16)
        for e in range(2):
            outs[2][e] = acc_s[2, :, e * ff : (e + 1) * ff].T.astype(BF16)

    if own:
        lane = lax.broadcasted_iota(jnp.int32, (rows, LANES), 1)
        term = jnp.zeros((rows, LANES), F32)
        shared = jnp.zeros((rows, LANES), F32)
        for j in range(2):
            sens = jnp.sum(sacc[j], axis=1, keepdims=True)
            term = term + jnp.where(lane == first_expert + j, sens, 0.0)
            shared = shared + gb[j] * sens
        grad = a_s[...] * (term - shared)
        high = grad.astype(BF16)
        low = (grad - high.astype(F32)).astype(BF16)
        gu[:, 2 * both : 2 * both + LANES] = high
        gu[:, 2 * both + LANES :] = low
        n_out = rp_out.shape[0]
        split = gu[:, 2 * both :]
        terms = mm(split, x_s[:, :width], TN)
        rp_out[...] = terms[:n_out] + terms[LANES : LANES + n_out]

        def mix(c, carry):
            here = pl.ds(pl.multiple_of(c * chunk_rows, chunk_rows), chunk_rows)
            o_s[here, :] = mm(hid[here, :], wd_s[...], NN).astype(BF16)
            return carry

        def token(c, carry):
            here = pl.ds(pl.multiple_of(c * chunk_rows, chunk_rows), chunk_rows)
            x_s[here, :width] = mm(gu[here, :], wc_s[...], NT).astype(BF16)
            return carry

        finals = []
        for place, (step, kept) in enumerate(((mix, o_s), (token, x_s))):
            lax.fori_loop(0, rows // chunk_rows, step, 0)
            for j in range(2):
                half = pl.ds(j * rows // 2, rows // 2)
                copy = pltpu.make_async_copy(
                    kept.at[half, pl.ds(0, width)], part_outs[2 * place + j], sems.at[out_sem + 3 + 2 * place + j]
                )
                copy.start()
                finals.append(copy)
        for copy in finals:
            copy.wait()
    if not last:
        for i in range(3):
            pltpu.make_async_copy(acc_s.at[i], outs[0].at[i], sems.at[out_sem + i]).wait()


def expert_call(own, last, scal, blocks, wc, wd, acc, n_experts):
    tok = sum(b.shape[0] for b in blocks) // (2 * PLANE)
    units = tuple(b.shape[0] // (2 * tok) for b in blocks)
    both, width = wd.shape
    ff = both // 2
    cols = width // lax.axis_size("dp")
    rows = PLANE * tok
    anywhere = pl.BlockSpec(memory_space=pl.ANY)
    vmem = pl.BlockSpec(memory_space=pltpu.VMEM)
    args = [*blocks, wc, wd]
    if not own:
        args.append(acc)
    if last:
        out_shape = [jax.ShapeDtypeStruct((2, cols, ff), BF16)] * 2 + [jax.ShapeDtypeStruct((2, ff, cols), BF16)]
        out_specs = [vmem] * 3
    else:
        out_shape = [jax.ShapeDtypeStruct((3, cols, both), F32)]
        out_specs = [anywhere]
    if own:
        out_shape += [
            *[jax.ShapeDtypeStruct((rows // 2, width), BF16)] * 4,
            jax.ShapeDtypeStruct((n_experts, width), F32),
        ]
        out_specs += [anywhere] * 4 + [vmem]
    chunk = rows // 4
    scratch = [
        pltpu.VMEM((rows, width + LANES), BF16),
        pltpu.VMEM((rows, width), BF16),
        pltpu.VMEM((width, 2 * both + LANES + LANES * own), BF16),
        pltpu.VMEM((both, width), BF16),
        pltpu.VMEM((chunk, 2 * both + LANES), F32),
        pltpu.VMEM((rows, both), F32),
        pltpu.VMEM((2, rows, LANES), F32),
        pltpu.VMEM((3, cols, both), F32),
    ]
    if own:
        scratch += [pltpu.VMEM((rows, LANES), F32), pltpu.VMEM((2, rows, LANES), F32)]
    scratch += [pltpu.VMEM((rows, both), BF16), pltpu.VMEM((rows, 2 * both + 2 * LANES * own), BF16)]
    scratch.append(pltpu.SemaphoreType.DMA((2 * PLANE + 11,)))
    aliases = {} if own or last else {1 + len(blocks) + 2: 0}
    flops = 2 * rows * width * both * 3 + 2 * rows * cols * both * 3
    return pl.pallas_call(
        functools.partial(expert_kernel, own, last, tok, width, ff, cols, units),
        grid_spec=pltpu.PrefetchScalarGridSpec(
            num_scalar_prefetch=1,
            grid=(),
            in_specs=[anywhere] * len(args),
            out_specs=out_specs,
            scratch_shapes=scratch,
        ),
        out_shape=out_shape,
        input_output_aliases=aliases,
        compiler_params=pltpu.CompilerParams(vmem_limit_bytes=58 * 1024 * 1024),
        cost_estimate=pl.CostEstimate(flops=flops, bytes_accessed=40_000_000, transcendentals=rows * both),
        name="experts_own" if own else "experts_last" if last else "experts_mid",
    )(scal, *args)


def flip(x, even, odd):
    groups = lax.axis_size("expert")
    return lax.ppermute(x, "expert", [(i, i ^ (odd if i % 2 else even)) for i in range(groups)])


def dense_body(tokens, expert_ids, router, w_gate, w_up, w_down, out_grad):
    tok, width = tokens.shape
    n_experts = router.shape[1]
    ff = w_gate.shape[2]
    n_dp = lax.axis_size("dp")
    me = lax.axis_index("expert")
    core = me % 2
    ladder = jnp.arange(LANES, dtype=jnp.int32)
    mask = jnp.any(expert_ids[:, :, None] == ladder[None, None, :], axis=1).astype(BF16)
    block = jnp.concatenate(
        [
            jnp.concatenate([tokens, mask], axis=1),
            jnp.concatenate([out_grad, jnp.zeros((tok, LANES), BF16)], axis=1),
        ],
        axis=0,
    )
    router_pad = jnp.pad(router, ((0, 0), (0, LANES - n_experts)))
    wc = jnp.concatenate([w_gate[0], w_gate[1], w_up[0], w_up[1], router_pad, router_pad], axis=1)
    wd = w_down.reshape(2 * ff, width)
    near_at = jnp.where(core == 0, 1, 2)
    scal = jnp.stack(
        [me * 2, lax.axis_index("dp"), 0, 4, near_at, near_at + 4, 7 - near_at, 3 - near_at, 3, 7]
    ).astype(jnp.int32)
    ring = [(i, (i + 1) % n_dp) for i in range(n_dp)]

    def swap(b):
        return flip(b, 1, 1)

    def pair_of(b):
        return jnp.concatenate([b, swap(b)], axis=0)

    def over_link(b):
        return flip(b, 2, 4)

    def onward(near):
        return flip(near[: 2 * tok], 4, 2)

    def along(b):
        return lax.ppermute(b, "dp", ring)

    def against(b):
        return lax.ppermute(b, "dp", [(j, i) for i, j in ring])

    def hold(*values):
        return lax.optimization_barrier(values)

    def experts(g, acc, blocks):
        return expert_call(g == 0, g == n_dp - 1, scal, blocks, wc, wd, acc, n_experts)

    def rows_of(x, j):
        return x[j * tok : (j + 1) * tok].astype(F32)

    def core_sums(low, other):
        return [rows_of(low, 0) + rows_of(other, 0)] + [
            (rows_of(low, j) + rows_of(other, j)).astype(BF16) for j in range(1, 4)
        ]

    def plane_total(mine, arrived):
        for a in arrived:
            mine = mine + a.astype(F32)
        return mine.astype(BF16)

    one = along(block)
    two_x, two_o = against(block[:tok]), against(block[tok:])
    pair0 = pair_of(block)
    near0 = over_link(pair0)
    near0, one, wc = hold(near0, one, wc)
    diag0, other0, pair1 = onward(near0), swap(near0), pair_of(one)
    diag0, other0, one, pair1, two_x = hold(diag0, other0, one, pair1, two_x)
    blocks0 = [pair0, near0, other0, diag0, swap(diag0)]

    near1, diag1 = over_link(pair1), along(diag0)
    three, sibling2 = along(one), swap(two_x)
    acc, mixed_low, mixed_high, token_low, token_high, rp = experts(0, None, blocks0)
    acc, mixed_low, mixed_high, token_low, token_high, rp, near1, diag1, two_o, three, sibling2 = hold(
        acc, mixed_low, mixed_high, token_low, token_high, rp, near1, diag1, two_o, three, sibling2
    )
    blocks1 = [pair1, near1, swap(near1), diag1, swap(diag1)]

    pair2 = jnp.concatenate([two_x, two_o, sibling2, swap(two_o)], axis=0)
    near2, diag2 = over_link(pair2), against(diag0)
    pair3 = pair_of(three)
    rp = rp + swap(rp)
    rp_z = lax.ppermute(rp, "dp", [(i, i ^ 1) for i in range(n_dp)])
    mixed_other, token_other = swap(mixed_high), swap(token_high)
    (acc,) = experts(1, acc, blocks1)
    acc, near2, diag2, pair3, rp, rp_z, mixed_other, token_other, mixed_low, token_low = hold(
        acc, near2, diag2, pair3, rp, rp_z, mixed_other, token_other, mixed_low, token_low
    )
    blocks2 = [pair2, near2, swap(near2), diag2, swap(diag2)]

    rp = rp + rp_z
    rp_z = lax.ppermute(rp, "dp", [(i, i ^ 2) for i in range(n_dp)])
    near3, diag3 = over_link(pair3), along(diag1)
    mixed_sums = core_sums(mixed_low, mixed_other)
    mixed_x, mixed_y = flip(mixed_sums[1], 2, 2), flip(mixed_sums[2], 4, 4)
    (acc,) = experts(2, acc, blocks2)
    acc, near3, diag3, mixed_x, mixed_y, rp, rp_z, mixed_d, token_low, token_other = hold(
        acc, near3, diag3, mixed_x, mixed_y, rp, rp_z, mixed_sums[3], token_low, token_other
    )

    rp = rp + rp_z
    rp_x = flip(rp, 2, 2)
    token_sums = core_sums(token_low, token_other)
    mixed_d = flip(mixed_d, 6, 6)
    token_parts = [flip(t, k, k) for t, k in zip(token_sums[1:], (2, 4, 6))]
    out = experts(3, acc, [pair3, near3, swap(near3), diag3, swap(diag3)])
    *out, rp, rp_x, mixed_d, token_x, token_y, token_d = hold(*out, rp, rp_x, mixed_d, *token_parts)
    rp = rp + rp_x
    rp_y = flip(rp, 4, 4)
    mixed = plane_total(mixed_sums[0], (mixed_x, mixed_y, mixed_d))
    token_grad = plane_total(token_sums[0], (token_x, token_y, token_d))
    rp = rp + rp_y
    return (mixed, token_grad, rp.T, *out)


def flat_rows(array):
    return array.reshape(array.shape[0], array.shape[1] * array.shape[2], array.shape[3])


def sparse_body(tokens, expert_ids, router, w_gate, w_up, w_down, out_grad):
    f32 = jnp.float32
    bf16 = jnp.bfloat16
    tok_dev, width = tokens.shape
    top = expert_ids.shape[1]
    n_experts = router.shape[1]
    local_experts = w_gate.shape[0]
    groups = lax.axis_size("expert")
    capacity = (tok_dev * top * 9 + 8 * n_experts - 1) // (8 * n_experts)
    n_assign = tok_dev * top
    flat_ids = expert_ids.reshape(-1)
    ladder = jnp.arange(n_experts, dtype=jnp.int32)
    onehot = (flat_ids[:, None] == ladder[None, :]).astype(jnp.int32)
    rank = jnp.sum((jnp.cumsum(onehot, axis=0) - onehot) * onehot, axis=1)
    owner = flat_ids // local_experts
    within = flat_ids % local_experts
    dest = (within * groups + owner) * capacity + rank
    slot_src = jnp.full((n_experts * capacity,), n_assign, jnp.int32)
    slot_src = slot_src.at[dest].set(jnp.arange(n_assign, dtype=jnp.int32))
    live = slot_src < n_assign
    slot_tok = jnp.where(live, slot_src // top, 0)
    logits = jnp.dot(tokens, router, preferred_element_type=f32)
    scores = jax.nn.sigmoid(logits)
    chosen = jnp.take_along_axis(scores, expert_ids, axis=1)
    total = jnp.sum(chosen, axis=1, keepdims=True)
    gates = chosen / total
    gate_slots = jnp.where(live, gates.reshape(-1)[jnp.minimum(slot_src, n_assign - 1)], 0.0)
    send = jnp.where(live[:, None], tokens[slot_tok], jnp.zeros((), bf16))
    send = send.reshape(local_experts, groups, capacity, width)
    piece = lax.all_to_all(send, "expert", split_axis=1, concat_axis=1, tiled=True)
    shape = piece.shape
    rows = flat_rows(piece)
    pre_gate = jnp.einsum("jrd,jdf->jrf", rows, w_gate, preferred_element_type=f32)
    pre_up = jnp.einsum("jrd,jdf->jrf", rows, w_up, preferred_element_type=f32)
    hidden = (pre_gate * jax.nn.sigmoid(pre_gate) * pre_up).astype(bf16)
    expert_out = jnp.einsum("jrf,jfd->jrd", hidden, w_down, preferred_element_type=f32).astype(bf16)
    hid_shape = (shape[0], shape[1], shape[2], hidden.shape[2])
    expert_out = expert_out.reshape(shape)
    hidden = hidden.reshape(hid_shape)
    results = (expert_out, hidden, piece, pre_gate.reshape(hid_shape), pre_up.reshape(hid_shape))
    expert_out = results[0]
    hidden = flat_rows(results[1])
    back = lax.all_to_all(expert_out, "expert", split_axis=1, concat_axis=1, tiled=True).reshape(
        n_experts * capacity, width
    )
    picked = back[dest].reshape(tok_dev, top, width)
    mixed = jnp.einsum("tk,tkd->td", gates, picked.astype(f32)).astype(bf16)
    gate_sens = jnp.einsum("tkd,td->tk", picked, out_grad, preferred_element_type=f32)
    grad_rows = (gate_slots[:, None] * out_grad[slot_tok].astype(f32)).astype(bf16)
    grad_send = jnp.where(live[:, None], grad_rows, jnp.zeros((), bf16))
    grad_send = grad_send.reshape(local_experts, groups, capacity, width)
    grad_in4 = lax.all_to_all(grad_send, "expert", split_axis=1, concat_axis=1, tiled=True)
    grad_in = flat_rows(grad_in4)
    pre_gate = flat_rows(results[3])
    pre_up = flat_rows(results[4])
    hidden_grad = jnp.einsum("jrd,jfd->jrf", grad_in, w_down, preferred_element_type=f32)
    sig = jax.nn.sigmoid(pre_gate)
    silu_val = pre_gate * sig
    gate_term = (hidden_grad * pre_up * sig * (1.0 + pre_gate * (1.0 - sig))).astype(bf16)
    up_term = (hidden_grad * silu_val).astype(bf16)
    input_grad = (
        jnp.einsum("jrf,jdf->jrd", gate_term, w_gate, preferred_element_type=f32)
        + jnp.einsum("jrf,jdf->jrd", up_term, w_up, preferred_element_type=f32)
    ).astype(bf16)
    input_grad = input_grad.reshape(grad_in4.shape)
    returned = lax.all_to_all(
        input_grad, "expert", split_axis=1, concat_axis=1, tiled=True
    ).reshape(n_experts * capacity, width)
    moe_grad = jnp.sum(returned[dest].reshape(tok_dev, top, width).astype(f32), axis=1)
    chosen_grad = (gate_sens - jnp.sum(gate_sens * gates, axis=1, keepdims=True)) / total
    sel_grad = chosen_grad * chosen * (1.0 - chosen)
    pick = (expert_ids[:, :, None] == ladder[None, None, :]).astype(f32)
    logit_grad = jnp.einsum("tk,tke->te", sel_grad, pick).astype(bf16)
    token_grad = (moe_grad + jnp.dot(logit_grad, router.T, preferred_element_type=f32)).astype(bf16)
    router_grad = lax.psum(
        jnp.dot(tokens.T, logit_grad, preferred_element_type=f32), ("expert", "dp")
    )
    hidden_width = hidden.shape[2]
    arrived4 = results[2]
    columns = (
        lax.all_to_all(arrived4, "dp", split_axis=3, concat_axis=1, tiled=True),
        lax.all_to_all(grad_in4, "dp", split_axis=3, concat_axis=1, tiled=True),
    )
    hid_shape = (local_experts, groups, capacity, hidden_width)
    hiddens = (
        lax.all_gather(gate_term.reshape(hid_shape), "dp", axis=1, tiled=True),
        lax.all_gather(up_term.reshape(hid_shape), "dp", axis=1, tiled=True),
        lax.all_gather(results[1], "dp", axis=1, tiled=True),
    )
    x_cols = flat_rows(columns[0])
    g_cols = flat_rows(columns[1])
    gate_grad = jnp.einsum(
        "jrd,jrf->jdf", x_cols, flat_rows(hiddens[0]), preferred_element_type=f32
    ).astype(bf16)
    up_grad = jnp.einsum(
        "jrd,jrf->jdf", x_cols, flat_rows(hiddens[1]), preferred_element_type=f32
    ).astype(bf16)
    down_grad = jnp.einsum(
        "jrf,jrd->jfd", flat_rows(hiddens[2]), g_cols, preferred_element_type=f32
    ).astype(bf16)
    return (mixed, token_grad, router_grad, gate_grad, up_grad, down_grad)


def body(*args):
    plane = lax.axis_size("expert") == 8 and args[3].shape[0] == 2
    line = lax.axis_size("dp")
    return (dense_body if plane and line == 4 else sparse_body)(*args)


def solution(mesh):
    placed = (
        P(("expert", "dp"), None),
        P(("expert", "dp"), None),
        P(),
        P("expert", None, None),
        P("expert", None, None),
        P("expert", None, None),
        P(("expert", "dp"), None),
    )
    return jax.shard_map(
        body,
        mesh=mesh,
        in_specs=placed,
        out_specs=(
            P(("expert", "dp"), None),
            P(("expert", "dp"), None),
            P(),
            P("expert", "dp", None),
            P("expert", "dp", None),
            P("expert", None, "dp"),
        ),
        check_vma=False,
    )
```
